32 devices in a mesh: groups: 2 (over x), replica: 8 (over z, y), channel: 2 (over core).
Axes of the slice: x: 2, y: 2, z: 4, core: 2. Of those that a mesh axis runs over, the one named last changes fastest.
Arguments:
- queries: bfloat16 [16, 2, 32, 4096], P(('groups', 'replica'), None, None, 'channel'), parts along dimension 0, may hold values from -360 to 360
- new_kv: bfloat16 [16, 2, 32, 1024], P(('groups', 'replica'), None, None, 'channel'), parts along dimension 0, may hold values from -6 to 6
- cached_lookup_pairs: bfloat16 [16, 1024, 1024], P(('groups', 'replica'), None, 'channel'), parts along dimension 0, may hold values from -6 to 6
- prefix_ssm: bfloat16 [16, 16, 8192], P(('groups', 'replica'), None, 'channel'), parts along dimension 0, may hold values from -6 to 6
- prefix_conv: bfloat16 [16, 3, 8192], P(('groups', 'replica'), None, 'channel'), parts along dimension 0, may hold values from -6 to 6
- pool_kv: bfloat16 [16, 4, 256, 1024], P(('groups', 'replica'), None, None, 'channel'), parts along dimension 0, may hold values from -6 to 6
- pool_ssm: bfloat16 [16, 16, 8192], P(('groups', 'replica'), None, 'channel'), parts along dimension 0, may hold values from -6 to 6
- pool_conv: bfloat16 [16, 3, 8192], P(('groups', 'replica'), None, 'channel'), parts along dimension 0, may hold values from -6 to 6
- owner_id: int32 [2], P('groups'), parts along dimension 0, may hold values from 0 to 7
- readers: int32 [16], P(('groups', 'replica')), parts along dimension 0, may hold values 0 or 1
- restore_src: int32 [16, 4], P('groups'), parts along dimension 0, may hold values from 0 to 7, as said below
- restore_blk: int32 [16, 4], P('groups'), parts along dimension 0, may hold values from 0 to 3, as said below
- state_src: int32 [16], P('groups'), parts along dimension 0, may hold values from 0 to 7, as said below
- ctx_blocks: int32 [16], P(('groups', 'replica')), parts along dimension 0, may hold values from 1 to 4, as said below
- mamba_x: bfloat16 [16, 2, 32, 8192], P(('groups', 'replica'), None, None, 'channel'), parts along dimension 0, may hold values from -6 to 6
- mamba_z: bfloat16 [16, 2, 32, 8192], P(('groups', 'replica'), None, None, 'channel'), parts along dimension 0, may hold values from -6 to 6
- mamba_dt: bfloat16 [16, 2, 32, 8192], P(('groups', 'replica'), None, None, 'channel'), parts along dimension 0, may hold values from -2 to 8
- dt_bias: float32 [8192], P('channel'), may hold values from -6 to -2.5
- a_log: float32 [16, 8192], P(None, 'channel'), may hold values from 0 to 2
- bypass_gain: float32 [8192], P('channel'), may hold values from 0.5 to 1.5
- conv_w: float32 [4, 8192], P(None, 'channel'), may hold values from -3 to 3
- conv_b: float32 [8192], P('channel'), may hold values from -0.5 to 0.5
- w_bc: bfloat16 [8192, 32], P('channel'), may hold values from -0.0625 to 0.0625
Outputs:
- attention_out: bfloat16 [16, 2, 32, 4096], P(('groups', 'replica'), None, None, 'channel'), parts along dimension 0
- mamba_out: bfloat16 [16, 2, 32, 8192], P(('groups', 'replica'), None, None, 'channel'), parts along dimension 0
The draws below stay inside these ranges and needn't reach their ends.
There are 2 independent parts, one for each index of `groups`. The reference program is written for one: setup_inputs(seed, part) draws one part's arguments, and reference() takes and returns one part's arrays. A program takes and returns all parts, laid end to end along the dimension named above; an argument that names none is the same for every part. Nothing has to cross between parts.
Inputs may be any that keep to these rules, and one draw needn't show every extreme that they name: `restore_src`: each row names 4 different replicas, and each replica is named in exactly 4 rows, so at most one block goes from one replica to one row's replica. Every pair (restore_src, restore_blk) is different: each stored block of each replica is listed exactly once. `state_src`: A permutation of the replicas. Only slots j < ctx_blocks[d] of row d are read; some replica has 4.
All inputs are finite; a program needn't handle non-finite values. No bound on the sum of `readers` on one device may be relied on, other than what follows from the above.
Results may differ from the reference program's by a relative error of at most 0.0049.
Values may be sent and summed in bfloat16 or wider, within the bound.
A program may use at most 128 MiB of HBM per device.

```python
import jax
import jax.numpy as jnp
from jax import lax

HD = 128
KV_HEADS = 4
Q_PER_KV = 8
Q_HEADS = 32
KVW = 1024
INNER = 8192
STATE = 16
CONV = 4
BLOCK = 256
MAXB = 4
POOL = 4
PREFIX = 1024
NEW = 32
N_REPLICA = 8


def restore_tables(key):
    base = jax.random.fold_in(key, 7031)
    key_a, key_b, key_c, key_d = jax.random.split(base, 4)
    labels = jax.random.permutation(key_a, N_REPLICA)
    slots = jax.random.permutation(key_b, N_REPLICA)
    offsets = jax.random.permutation(key_c, N_REPLICA)[:MAXB]
    sources = labels[(slots[:, None] + offsets[None, :]) % N_REPLICA]
    orders = jax.vmap(lambda sub_key: jax.random.permutation(sub_key, MAXB))(jax.random.split(key_d, N_REPLICA))
    blocks = orders[sources, jnp.arange(MAXB)[None, :]]
    return (sources.astype(jnp.int32), blocks.astype(jnp.int32))


def draw_restore_src(key, part):
    return restore_tables(key)[0]


def draw_restore_blk(key, part):
    return restore_tables(key)[1]


def draw_state_src(key, part):
    return jax.random.permutation(jax.random.fold_in(key, 9127), N_REPLICA).astype(jnp.int32)


def draw_ctx_blocks(key, part):
    base = jax.random.fold_in(key, 4409)
    key_a, key_b = jax.random.split(base)
    payload_lines = jax.random.randint(key_a, (N_REPLICA,), MAXB - 3, MAXB + 1)
    chosen = jax.random.randint(key_b, (), 0, N_REPLICA)
    return jnp.where(jnp.arange(N_REPLICA) == chosen, MAXB, payload_lines).astype(jnp.int32)


def draw_queries(key, part):
    base = jax.random.fold_in(key, 2203)
    key_a = jax.random.fold_in(base, 0)
    payload_lines = jnp.clip(jax.random.normal(key_a, (N_REPLICA, 2, NEW, Q_HEADS * HD), jnp.float32), -6.0, 6.0)
    return payload_lines.astype(jnp.bfloat16)


def draw_mamba_dt(key, part):
    base = jax.random.fold_in(key, 5581)
    key_a, key_b = jax.random.split(base)
    shape = (N_REPLICA, 2, NEW, INNER)
    payload_lines = jnp.clip(0.5 * jax.random.normal(key_a, shape, jnp.float32), -2.0, 2.0)
    destination_places = jax.random.randint(key_b, (N_REPLICA, 2, 3), 0, NEW)
    update_order = jnp.arange(NEW)[None, None, None, :]
    copy_batches = jnp.sum((destination_places[..., None] == update_order).astype(jnp.float32), axis=2)
    return (payload_lines + 2.0 * copy_batches[..., None]).astype(jnp.bfloat16)


def plant(entries, rng, low, largest):
    longest = entries.shape.index(max(entries.shape))
    spots = []
    for shift in (0, 1):
        where = [jax.random.randint(jax.random.fold_in(rng, axis), (), 0, length) for axis, length in enumerate(entries.shape)]
        where[longest] = (where[longest] + shift) % entries.shape[longest]
        spots.append(tuple(where))
    return entries.at[spots[0]].set(low).at[spots[1]].set(largest)


def block_levels(own_key, shape, cuts, low, largest):
    loudness, own = 1.0, jax.random.fold_in(own_key, 6)
    for position, blocks in cuts:
        steps = jnp.exp(jax.random.uniform(jax.random.fold_in(own, position), (blocks,), jnp.float32, low / len(cuts), largest / len(cuts)))
        loudness = loudness * jnp.repeat(steps, shape[position] // blocks).reshape([-1 if axis == position else 1 for axis in range(len(shape))])
    return loudness


def noise(key, extent, deviation, limit, shards=(), kind=jnp.bfloat16):
    factor_of = block_levels(key, extent, shards, -0.22, 0.18) if shards else 1.0
    values = jax.random.normal(key, extent, jnp.float32) * deviation * factor_of
    return jnp.minimum(jnp.maximum(values, -limit), limit).astype(kind)


def setup_inputs(seed: int = 0, part: int = 0) -> dict:
    seeds = jax.random.split(jax.random.key(seed), 24)
    part_keys = jax.random.split(jax.random.fold_in(seeds[23], part), 24)
    queries = draw_queries(jax.random.fold_in(jax.random.fold_in(seeds[23], part), 71), part)
    new_kv = noise(part_keys[1], (N_REPLICA, 2, NEW, KVW), 1.0, 6.0, ((0, 8), (3, 2)))
    cached_lookup_pairs = noise(part_keys[2], (N_REPLICA, PREFIX, KVW), 1.0, 6.0, ((0, 8), (2, 2)))
    prefix_ssm = noise(part_keys[3], (N_REPLICA, STATE, INNER), 1.0, 6.0, ((0, 8), (2, 2)))
    prefix_conv = noise(part_keys[4], (N_REPLICA, CONV - 1, INNER), 1.0, 6.0, ((0, 8), (2, 2)))
    pool_kv = noise(part_keys[5], (N_REPLICA, POOL, BLOCK, KVW), 1.0, 6.0, ((0, 8), (3, 2)))
    pool_ssm = noise(part_keys[6], (N_REPLICA, STATE, INNER), 1.0, 6.0, ((0, 8), (2, 2)))
    pool_conv = noise(part_keys[7], (N_REPLICA, CONV - 1, INNER), 1.0, 6.0, ((0, 8), (2, 2)))
    owner_id = jax.random.randint(part_keys[8], (1,), 0, N_REPLICA).astype(jnp.int32)
    readers = plant((jax.random.randint(part_keys[9], (N_REPLICA,), 0, 4) < 3).astype(jnp.int32), jax.random.fold_in(part_keys[9], 1), 0, 1)
    restore_src = draw_restore_src(jax.random.fold_in(jax.random.fold_in(seeds[23], part), 71), part)
    restore_blk = draw_restore_blk(jax.random.fold_in(jax.random.fold_in(seeds[23], part), 71), part)
    state_src = draw_state_src(jax.random.fold_in(jax.random.fold_in(seeds[23], part), 71), part)
    ctx_blocks = draw_ctx_blocks(jax.random.fold_in(jax.random.fold_in(seeds[23], part), 71), part)
    mamba_x = noise(part_keys[14], (N_REPLICA, 2, NEW, INNER), 1.0, 6.0, ((0, 8), (3, 2)))
    mamba_z = noise(part_keys[15], (N_REPLICA, 2, NEW, INNER), 1.0, 6.0, ((0, 8), (3, 2)))
    mamba_dt = draw_mamba_dt(jax.random.fold_in(jax.random.fold_in(seeds[23], part), 71), part)
    dt_bias = jnp.clip(-6.0 + 3.5 * jax.random.uniform(seeds[17], (INNER,), jnp.float32) ** block_levels(seeds[17], (INNER,), ((0, 2),), -0.2, 0.2), -6.0, -2.5)
    a_log = jnp.clip(2.0 * jax.random.uniform(seeds[18], (STATE, INNER), jnp.float32) ** block_levels(seeds[18], (STATE, INNER), ((1, 2),), -0.2, 0.2), 0.0, 2.0)
    bypass_gain = jnp.clip(0.5 + 1.0 * jax.random.uniform(seeds[19], (INNER,), jnp.float32) ** block_levels(seeds[19], (INNER,), ((0, 2),), -0.2, 0.2), 0.5, 1.5)
    conv_w = noise(seeds[20], (CONV, INNER), CONV ** -0.5, 3.0, ((1, 2),), jnp.float32)
    conv_b = jnp.clip(jax.random.uniform(seeds[21], (INNER,), jnp.float32, -0.5, 0.5) * block_levels(seeds[21], (INNER,), ((0, 2),), -0.4, 0.0), -0.5, 0.5)
    w_bc = noise(seeds[22], (INNER, 2 * STATE), INNER ** -0.5, 0.0625, ((0, 2),))
    return {"queries": queries, "new_kv": new_kv, "cached_lookup_pairs": cached_lookup_pairs, "prefix_ssm": prefix_ssm, "prefix_conv": prefix_conv, "pool_kv": pool_kv, "pool_ssm": pool_ssm, "pool_conv": pool_conv, "owner_id": owner_id, "readers": readers, "restore_src": restore_src, "restore_blk": restore_blk, "state_src": state_src, "ctx_blocks": ctx_blocks, "mamba_x": mamba_x, "mamba_z": mamba_z, "mamba_dt": mamba_dt, "dt_bias": dt_bias, "a_log": a_log, "bypass_gain": bypass_gain, "conv_w": conv_w, "conv_b": conv_b, "w_bc": w_bc}


def attend(query_rows, context, live_keys, fresh_keys):
    factor = query_rows.shape[-1] ** -0.5
    rows_f = query_rows.astype(jnp.float32)
    scores_ctx = jnp.einsum("qhgd,khd->hgqk", rows_f, context[:, :, 0].astype(jnp.float32)) * factor
    scores_ctx = jnp.where(live_keys, scores_ctx, -jnp.inf)
    scores_new = jnp.einsum("qhgd,khd->hgqk", rows_f, fresh_keys[:, :, 0].astype(jnp.float32)) * factor
    new_count = fresh_keys.shape[0]
    causal = lax.broadcasted_iota(jnp.int32, (new_count, new_count), 0) >= lax.broadcasted_iota(jnp.int32, (new_count, new_count), 1)
    scores_new = jnp.where(causal, scores_new, -jnp.inf)
    highest = jnp.maximum(jnp.max(scores_ctx, axis=-1, keepdims=True), jnp.max(scores_new, axis=-1, keepdims=True))
    weight_ctx = jnp.exp(scores_ctx - highest)
    weight_new = jnp.exp(scores_new - highest)
    denominator = jnp.sum(weight_ctx, axis=-1) + jnp.sum(weight_new, axis=-1)
    scaled_product = jnp.einsum("hgqk,khd->qhgd", weight_ctx.astype(jnp.bfloat16).astype(jnp.float32), context[:, :, 1].astype(jnp.float32))
    scaled_product = scaled_product + jnp.einsum("hgqk,khd->qhgd", weight_new.astype(jnp.bfloat16).astype(jnp.float32), fresh_keys[:, :, 1].astype(jnp.float32))
    result = scaled_product / jnp.transpose(denominator, (2, 0, 1))[..., None]
    return result.astype(jnp.bfloat16).reshape(new_count, -1)


def reference(queries, new_kv, cached_lookup_pairs, prefix_ssm, prefix_conv, pool_kv, pool_ssm, pool_conv, owner_id, readers, restore_src, restore_blk, state_src, ctx_blocks, mamba_x, mamba_z, mamba_dt, dt_bias, a_log, bypass_gain, conv_w, conv_b, w_bc):
    owner_pos = owner_id[0]
    shared_kv = cached_lookup_pairs[owner_pos]
    shared_ssm = prefix_ssm[owner_pos].astype(jnp.float32)
    shared_conv = prefix_conv[owner_pos].astype(jnp.float32)
    decay_rate = -jnp.exp(a_log)
    w_bc_f = w_bc.astype(jnp.float32)

    def serve_one(replica_pos):
        reading_replica = readers[replica_pos] > 0
        grouped = queries[replica_pos].reshape(2, NEW, KV_HEADS, Q_PER_KV, HD)
        fresh_kv = new_kv[replica_pos].reshape(2, NEW, KV_HEADS, 2, HD)
        prefix_ctx = shared_kv.reshape(PREFIX, KV_HEADS, 2, HD)
        fresh_out = attend(grouped[0], prefix_ctx, jnp.broadcast_to(reading_replica, (PREFIX,)), fresh_kv[0])
        sources = restore_src[replica_pos]
        blocks = restore_blk[replica_pos]
        restored = pool_kv[sources, blocks].reshape(MAXB * BLOCK, KV_HEADS, 2, HD)
        live_keys = jnp.arange(MAXB * BLOCK, dtype=jnp.int32) < ctx_blocks[replica_pos] * BLOCK
        resumed_out = attend(grouped[1], restored, live_keys, fresh_kv[1])
        holder = state_src[replica_pos]
        start_ssm = jnp.stack([jnp.where(reading_replica, shared_ssm, 0.0), pool_ssm[holder].astype(jnp.float32)])
        start_conv = jnp.stack([jnp.where(reading_replica, shared_conv, 0.0), pool_conv[holder].astype(jnp.float32)])
        padded = jnp.concatenate([start_conv, mamba_x[replica_pos].astype(jnp.float32)], axis=1)
        conv_sum = conv_b + conv_w[0] * padded[:, 0:NEW]
        for offset in range(1, CONV):
            conv_sum = conv_sum + conv_w[offset] * padded[:, offset:offset + NEW]
        signal = jax.nn.silu(conv_sum)
        signal_round = lax.optimization_barrier(signal.astype(jnp.bfloat16)).astype(jnp.float32)
        state_bc = jnp.einsum("rtc,cs->rts", signal_round, w_bc_f)
        input_gain = state_bc[..., :STATE]
        readout = state_bc[..., STATE:]
        step_size = jax.nn.softplus(mamba_dt[replica_pos].astype(jnp.float32) + dt_bias)

        def advance(hidden, inputs):
            step_now, signal_now, gain_now, readout_now = inputs
            hidden = jnp.exp(step_now[:, None, :] * decay_rate) * hidden + gain_now[:, :, None] * (step_now * signal_now)[:, None, :]
            result = jnp.sum(readout_now[:, :, None] * hidden, axis=1) + bypass_gain * signal_now
            return hidden, result

        ignored, outputs = lax.scan(advance, start_ssm, (jnp.swapaxes(step_size, 0, 1), jnp.swapaxes(signal, 0, 1), jnp.swapaxes(input_gain, 0, 1), jnp.swapaxes(readout, 0, 1)))
        gated = (jnp.swapaxes(outputs, 0, 1) * jax.nn.silu(mamba_z[replica_pos].astype(jnp.float32))).astype(jnp.bfloat16)
        return jnp.stack([fresh_out, resumed_out]), gated

    attention_out, mamba_out = lax.map(serve_one, jnp.arange(N_REPLICA, dtype=jnp.int32))
    return attention_out, mamba_out
```

```python
import jax
import jax.numpy as jnp
from jax import lax
from jax.experimental import pallas as pl
from jax.experimental.pallas import tpu as pltpu
from jax.sharding import PartitionSpec as P

HD = 128
Q_PER_KV = 8
CHUNK = 512


def from_root(value, axis, source):
    kept = jnp.where(lax.axis_index(axis) == source, value, 0).astype(value.dtype)
    return lax.psum(kept, axis)


def attend_kernel(parts, src_ref, live_ref, q_ref, *refs):
    ctx_refs, new_ref, out_ref = refs[:parts], refs[parts], refs[parts + 1]
    new_len = q_ref.shape[0]
    heads = new_ref.shape[1] // (2 * HD)
    factor = HD ** (-0.5)
    rows = Q_PER_KV * new_len
    live = live_ref[0]
    for head in range(heads):
        query = jnp.concatenate(
            [
                q_ref[:, (head * Q_PER_KV + g) * HD : (head * Q_PER_KV + g + 1) * HD]
                for g in range(Q_PER_KV)
            ],
            axis=0,
        )
        key_cols = slice(2 * head * HD, (2 * head + 1) * HD)
        value_cols = slice((2 * head + 1) * HD, (2 * head + 2) * HD)
        contract = (((1,), (1,)), ((), ()))
        scores = []
        start = 0
        for ref in ctx_refs:
            piece = (
                lax.dot_general(
                    query, ref[0, :, key_cols], contract, preferred_element_type=jnp.float32
                )
                * factor
            )
            position = start + lax.broadcasted_iota(jnp.int32, piece.shape, 1)
            scores.append(jnp.where(position < live, piece, -jnp.inf))
            start += ref.shape[1]
        fresh = (
            lax.dot_general(
                query, new_ref[:, key_cols], contract, preferred_element_type=jnp.float32
            )
            * factor
        )
        time = lax.rem(lax.broadcasted_iota(jnp.int32, fresh.shape, 0), new_len)
        fresh = jnp.where(
            time >= lax.broadcasted_iota(jnp.int32, fresh.shape, 1), fresh, -jnp.inf
        )
        highest = jnp.max(fresh, axis=1, keepdims=True)
        for piece in scores:
            highest = jnp.maximum(highest, jnp.max(piece, axis=1, keepdims=True))
        weight = jnp.exp(fresh - highest)
        total = jnp.sum(weight, axis=1, keepdims=True)
        mixed = jnp.dot(
            weight.astype(jnp.bfloat16),
            new_ref[:, value_cols],
            preferred_element_type=jnp.float32,
        )
        for piece, ref in zip(scores, ctx_refs):
            weight = jnp.exp(piece - highest)
            total = total + jnp.sum(weight, axis=1, keepdims=True)
            mixed = mixed + jnp.dot(
                weight.astype(jnp.bfloat16),
                ref[0, :, value_cols],
                preferred_element_type=jnp.float32,
            )
        result = (mixed / total).astype(out_ref.dtype)
        for g in range(Q_PER_KV):
            at = (head * Q_PER_KV + g) * HD
            out_ref[:, at : at + HD] = result[g * new_len : (g + 1) * new_len]


def attend(request, queries, blocks, source, live, new_kv):
    parts = source.shape[0]
    _, block_len, width = blocks.shape
    _, _, new_len, q_width = queries.shape

    def pick(j):
        return pl.BlockSpec((1, block_len, width), lambda i, s, l: (s[j], 0, 0))

    return pl.pallas_call(
        lambda *refs: attend_kernel(parts, *refs),
        grid_spec=pltpu.PrefetchScalarGridSpec(
            num_scalar_prefetch=2,
            grid=(1,),
            in_specs=[
                pl.BlockSpec((None, None, new_len, q_width), lambda i, s, l: (0, request, 0, 0))
            ]
            + [pick(j) for j in range(parts)]
            + [pl.BlockSpec((None, None, new_len, width), lambda i, s, l: (0, request, 0, 0))],
            out_specs=pl.BlockSpec((new_len, q_width), lambda i, s, l: (0, 0)),
        ),
        out_shape=jax.ShapeDtypeStruct((new_len, q_width), jnp.bfloat16),
        name="attend",
    )(source, live, queries, *([blocks] * parts), new_kv)


def signal_kernel(read_ref, x_ref, conv0_ref, conv1_ref, w_ref, b_ref, wbc_ref, sig_ref, bc_ref, pad):
    taps = w_ref.shape[0]
    new_len = x_ref.shape[1]
    reading = read_ref[0] > 0
    base = 8 - (taps - 1)
    first = jnp.where(reading, conv0_ref[...].astype(jnp.float32), 0.0)
    pad[0, base:8] = first
    pad[1, base:8] = conv1_ref[...].astype(jnp.float32)

    @pl.when(pl.program_id(0) == 0)
    def _():
        bc_ref[...] = jnp.zeros_like(bc_ref)

    for r in range(2):
        pad[r, 8 : 8 + new_len] = x_ref[r].astype(jnp.float32)
        total = b_ref[...] + w_ref[0:1] * pad[r, base : base + new_len]
        for k in range(1, taps):
            total = total + w_ref[k : k + 1] * pad[r, base + k : base + k + new_len]
        signal = total * jax.nn.sigmoid(total)
        sig_ref[r] = signal
        bc_ref[r] += jnp.dot(
            signal.astype(jnp.bfloat16), wbc_ref[...], preferred_element_type=jnp.float32
        )


def signal_call(reading, x, conv0, conv1, w, b, wbc):
    _, _, new_len, channels = x.shape
    taps, cols = w.shape[0], wbc.shape[1]
    chunk = CHUNK
    return pl.pallas_call(
        signal_kernel,
        grid_spec=pltpu.PrefetchScalarGridSpec(
            num_scalar_prefetch=1,
            grid=(channels // chunk,),
            in_specs=[
                pl.BlockSpec((None, 2, new_len, chunk), lambda i, s: (0, 0, 0, i)),
                pl.BlockSpec((taps - 1, chunk), lambda i, s: (0, i)),
                pl.BlockSpec((taps - 1, chunk), lambda i, s: (0, i)),
                pl.BlockSpec((taps, chunk), lambda i, s: (0, i)),
                pl.BlockSpec((1, chunk), lambda i, s: (0, i)),
                pl.BlockSpec((chunk, cols), lambda i, s: (i, 0)),
            ],
            out_specs=[
                pl.BlockSpec((2, new_len, chunk), lambda i, s: (0, 0, i)),
                pl.BlockSpec((2, new_len, cols), lambda i, s: (0, 0, 0)),
            ],
            scratch_shapes=[pltpu.VMEM((2, 8 + new_len, chunk), jnp.float32)],
        ),
        out_shape=[
            jax.ShapeDtypeStruct((2, new_len, channels), jnp.float32),
            jax.ShapeDtypeStruct((2, new_len, cols), jnp.float32),
        ],
        name="signal",
    )(reading, x, conv0, conv1, w, b, wbc)


def scan_kernel(
    read_ref, bc_ref, sig_ref, dt_ref, z_ref, bias_ref, alog_ref, gain_ref, s0_ref, s1_ref,
    out_ref, spread, step_buf, push_buf, scan_buf
):
    states, chunk = alog_ref.shape
    new_len = sig_ref.shape[1]

    @pl.when(pl.program_id(0) == 0)
    def _():
        for r in range(2):
            columns = bc_ref[r].T
            for t in range(new_len):
                spread[r, t] = jnp.broadcast_to(columns[:, t : t + 1], spread.shape[2:])

    decay = -jnp.exp(alog_ref[...])
    hidden = []
    for r in range(2):
        x = dt_ref[r].astype(jnp.float32) + bias_ref[...]
        step = jnp.maximum(x, 0.0) + jnp.log1p(jnp.exp(-jnp.abs(x)))
        step_buf[r] = step
        push_buf[r] = step * sig_ref[r]
    hidden = (
        jnp.where(read_ref[0] > 0, s0_ref[...].astype(jnp.float32), 0.0),
        s1_ref[...].astype(jnp.float32),
    )
    tiles = chunk // HD
    for t in range(new_len):
        state = []
        for r in range(2):
            now = jnp.broadcast_to(step_buf[r, t : t + 1], (states, chunk))
            push = jnp.broadcast_to(push_buf[r, t : t + 1], (states, chunk))
            both = spread[r, t]
            gain = jnp.concatenate([both[:states]] * tiles, axis=1)
            read = jnp.concatenate([both[states:]] * tiles, axis=1)
            new = jnp.exp(now * decay) * hidden[r] + gain * push
            scan_buf[r, t : t + 1] = jnp.sum(read * new, axis=0, keepdims=True)
            state.append(new)
        hidden = tuple(state)
    for r in range(2):
        z = z_ref[r].astype(jnp.float32)
        full = scan_buf[r] + gain_ref[...] * sig_ref[r]
        out_ref[r] = (full * (z * jax.nn.sigmoid(z))).astype(out_ref.dtype)


def scan_call(reading, bc, signal, dt, z, bias, alog, gain, s0, s1):
    _, new_len, channels = signal.shape
    states, cols = alog.shape[0], bc.shape[2]
    chunk = CHUNK
    row = pl.BlockSpec((1, chunk), lambda i, s: (0, i))
    state = pl.BlockSpec((states, chunk), lambda i, s: (0, i))
    seq = pl.BlockSpec((None, 2, new_len, chunk), lambda i, s: (0, 0, 0, i))
    return pl.pallas_call(
        scan_kernel,
        grid_spec=pltpu.PrefetchScalarGridSpec(
            num_scalar_prefetch=1,
            grid=(channels // chunk,),
            in_specs=[
                pl.BlockSpec((2, new_len, cols), lambda i, s: (0, 0, 0)),
                pl.BlockSpec((2, new_len, chunk), lambda i, s: (0, 0, i)),
                seq,
                seq,
                row,
                state,
                row,
                state,
                state,
            ],
            out_specs=pl.BlockSpec((None, 2, new_len, chunk), lambda i, s: (0, 0, 0, i)),
            scratch_shapes=[
                pltpu.VMEM((2, new_len, cols, HD), jnp.float32),
                pltpu.VMEM((2, new_len, chunk), jnp.float32),
                pltpu.VMEM((2, new_len, chunk), jnp.float32),
                pltpu.VMEM((2, new_len, chunk), jnp.float32),
            ],
        ),
        out_shape=jax.ShapeDtypeStruct((1, 2, new_len, channels), jnp.bfloat16),
        name="scan",
    )(reading, bc, signal, dt, z, bias, alog, gain, s0, s1)


def local(
    queries,
    new_kv,
    cached_lookup_pairs,
    prefix_ssm,
    prefix_conv,
    pool_kv,
    pool_ssm,
    pool_conv,
    owner_id,
    readers,
    restore_src,
    restore_blk,
    state_src,
    ctx_blocks,
    mamba_x,
    mamba_z,
    mamba_dt,
    dt_bias,
    a_log,
    bypass_gain,
    conv_w,
    conv_b,
    w_bc,
):
    block_len = pool_kv.shape[2]
    own_index = lax.axis_index("replica")
    shared_kv, shared_ssm, shared_conv = (
        from_root(cached_lookup_pairs, "replica", owner_id[0]),
        from_root(prefix_ssm, "replica", owner_id[0]),
        from_root(prefix_conv, "replica", owner_id[0]),
    )
    my_sources = lax.dynamic_index_in_dim(restore_src, own_index, 0, keepdims=False)
    my_holder = lax.dynamic_index_in_dim(state_src, own_index, 0, keepdims=False)
    matched = restore_src == own_index
    served = jnp.any(matched, axis=1)
    picked = jnp.sum(jnp.where(matched, restore_blk, 0), axis=1)
    send_kv = jnp.where(
        served[:, None, None], jnp.take(pool_kv[0], picked, axis=0), jnp.zeros((), pool_kv.dtype)
    )
    holder = (state_src == own_index)[:, None, None]
    send_ssm = jnp.where(holder, pool_ssm, jnp.zeros((), pool_ssm.dtype))
    send_conv = jnp.where(holder, pool_conv, jnp.zeros((), pool_conv.dtype))
    got_kv, got_ssm, got_conv = (
        lax.all_to_all(send_kv[:, None], "replica", split_axis=0, concat_axis=1, tiled=True),
        lax.all_to_all(send_ssm[:, None], "replica", split_axis=0, concat_axis=1, tiled=True),
        lax.all_to_all(send_conv[:, None], "replica", split_axis=0, concat_axis=1, tiled=True),
    )
    restored_ssm = lax.dynamic_index_in_dim(got_ssm[0], my_holder, 0, keepdims=False)
    restored_conv = lax.dynamic_index_in_dim(got_conv[0], my_holder, 0, keepdims=False)
    reading = (readers > 0).astype(jnp.int32)
    signal, partial_bc = signal_call(
        reading, mamba_x, shared_conv[0], restored_conv, conv_w, conv_b[None], w_bc
    )
    state_bc = lax.psum(partial_bc, "channel")
    mamba_out = scan_call(
        reading, state_bc, signal, mamba_dt, mamba_z, dt_bias[None], a_log, bypass_gain[None],
        shared_ssm[0], restored_ssm
    )
    prefix = shared_kv[0]
    parts = prefix.shape[0] // block_len
    prefix_blocks = prefix.reshape(parts, prefix.shape[0] // parts, prefix.shape[1])
    fresh_out = attend(
        0, queries, prefix_blocks, lax.iota(jnp.int32, parts), reading * prefix.shape[0], new_kv
    )
    resumed_out = attend(1, queries, got_kv[0], my_sources, ctx_blocks * block_len, new_kv)
    return (jnp.stack([fresh_out, resumed_out])[None], mamba_out)


def placed_specs():
    return (
        P(("groups", "replica"), None, None, "channel"),
        P(("groups", "replica"), None, None, "channel"),
        P(("groups", "replica"), None, "channel"),
        P(("groups", "replica"), None, "channel"),
        P(("groups", "replica"), None, "channel"),
        P(("groups", "replica"), None, None, "channel"),
        P(("groups", "replica"), None, "channel"),
        P(("groups", "replica"), None, "channel"),
        P("groups"),
        P(("groups", "replica")),
        P("groups", None),
        P("groups", None),
        P("groups"),
        P(("groups", "replica")),
        P(("groups", "replica"), None, None, "channel"),
        P(("groups", "replica"), None, None, "channel"),
        P(("groups", "replica"), None, None, "channel"),
        P("channel"),
        P(None, "channel"),
        P("channel"),
        P(None, "channel"),
        P("channel"),
        P("channel", None),
    )


def solution(mesh):
    return jax.shard_map(
        local,
        mesh=mesh,
        in_specs=placed_specs(),
        out_specs=(
            P(("groups", "replica"), None, None, "channel"),
            P(("groups", "replica"), None, None, "channel"),
        ),
        check_vma=False,
    )
```

```python
import jax
import jax.numpy as jnp
from jax import lax
from jax.experimental import pallas as pl
from jax.experimental.pallas import tpu as pltpu
from jax.sharding import PartitionSpec as P

HD = 128
Q_PER_KV = 8
CHUNK = 512


def attend_kernel(parts, src_ref, live_ref, q_ref, *refs):
    ctx_refs, new_ref, out_ref = refs[:parts], refs[parts], refs[parts + 1]
    new_len = q_ref.shape[0]
    heads = new_ref.shape[1] // (2 * HD)
    factor = HD ** (-0.5)
    rows = Q_PER_KV * new_len
    live = live_ref[0]
    for head in range(heads):
        query = jnp.concatenate(
            [
                q_ref[:, (head * Q_PER_KV + g) * HD : (head * Q_PER_KV + g + 1) * HD]
                for g in range(Q_PER_KV)
            ],
            axis=0,
        )
        key_cols = slice(2 * head * HD, (2 * head + 1) * HD)
        value_cols = slice((2 * head + 1) * HD, (2 * head + 2) * HD)
        contract = (((1,), (1,)), ((), ()))
        scores = []
        start = 0
        for ref in ctx_refs:
            piece = (
                lax.dot_general(
                    query, ref[0, :, key_cols], contract, preferred_element_type=jnp.float32
                )
                * factor
            )
            position = start + lax.broadcasted_iota(jnp.int32, piece.shape, 1)
            scores.append(jnp.where(position < live, piece, -jnp.inf))
            start += ref.shape[1]
        fresh = (
            lax.dot_general(
                query, new_ref[:, key_cols], contract, preferred_element_type=jnp.float32
            )
            * factor
        )
        time = lax.rem(lax.broadcasted_iota(jnp.int32, fresh.shape, 0), new_len)
        fresh = jnp.where(
            time >= lax.broadcasted_iota(jnp.int32, fresh.shape, 1), fresh, -jnp.inf
        )
        highest = jnp.max(fresh, axis=1, keepdims=True)
        for piece in scores:
            highest = jnp.maximum(highest, jnp.max(piece, axis=1, keepdims=True))
        weight = jnp.exp(fresh - highest)
        total = jnp.sum(weight, axis=1, keepdims=True)
        mixed = jnp.dot(
            weight.astype(jnp.bfloat16),
            new_ref[:, value_cols],
            preferred_element_type=jnp.float32,
        )
        for piece, ref in zip(scores, ctx_refs):
            weight = jnp.exp(piece - highest)
            total = total + jnp.sum(weight, axis=1, keepdims=True)
            mixed = mixed + jnp.dot(
                weight.astype(jnp.bfloat16),
                ref[0, :, value_cols],
                preferred_element_type=jnp.float32,
            )
        result = (mixed / total).astype(out_ref.dtype)
        for g in range(Q_PER_KV):
            at = (head * Q_PER_KV + g) * HD
            out_ref[:, at : at + HD] = result[g * new_len : (g + 1) * new_len]


def attend(request, queries, blocks, source, live, new_kv):
    parts = source.shape[0]
    _, block_len, width = blocks.shape
    _, _, new_len, q_width = queries.shape

    def pick(j):
        return pl.BlockSpec((1, block_len, width), lambda i, s, l: (s[j], 0, 0))

    return pl.pallas_call(
        lambda *refs: attend_kernel(parts, *refs),
        grid_spec=pltpu.PrefetchScalarGridSpec(
            num_scalar_prefetch=2,
            grid=(1,),
            in_specs=[
                pl.BlockSpec((None, None, new_len, q_width), lambda i, s, l: (0, request, 0, 0))
            ]
            + [pick(j) for j in range(parts)]
            + [pl.BlockSpec((None, None, new_len, width), lambda i, s, l: (0, request, 0, 0))],
            out_specs=pl.BlockSpec((new_len, q_width), lambda i, s, l: (0, 0)),
        ),
        out_shape=jax.ShapeDtypeStruct((new_len, q_width), jnp.bfloat16),
        name="attend",
    )(source, live, queries, *([blocks] * parts), new_kv)


def signal_kernel(read_ref, x_ref, state_ref, w_ref, b_ref, wbc_ref, sig_ref, bc_ref, pad):
    taps = w_ref.shape[0]
    new_len = x_ref.shape[1]
    reading = read_ref[0] > 0
    base = 8 - (taps - 1)
    both = state_ref[...].astype(jnp.float32)
    start = wbc_ref.shape[1] // 2
    pad[0, base:8] = jnp.where(reading, both[0, start : start + taps - 1], 0.0)
    pad[1, base:8] = both[1, start : start + taps - 1]

    @pl.when(pl.program_id(0) == 0)
    def _():
        bc_ref[...] = jnp.zeros_like(bc_ref)

    for r in range(2):
        pad[r, 8 : 8 + new_len] = x_ref[r].astype(jnp.float32)
        total = b_ref[...] + w_ref[0:1] * pad[r, base : base + new_len]
        for k in range(1, taps):
            total = total + w_ref[k : k + 1] * pad[r, base + k : base + k + new_len]
        signal = total * jax.nn.sigmoid(total)
        sig_ref[r] = signal
        bc_ref[r] += jnp.dot(
            signal.astype(jnp.bfloat16), wbc_ref[...], preferred_element_type=jnp.float32
        )


def signal_call(reading, x, states, w, b, wbc):
    _, _, new_len, channels = x.shape
    taps, cols = w.shape[0], wbc.shape[1]
    chunk = CHUNK
    return pl.pallas_call(
        signal_kernel,
        grid_spec=pltpu.PrefetchScalarGridSpec(
            num_scalar_prefetch=1,
            grid=(channels // chunk,),
            in_specs=[
                pl.BlockSpec((None, 2, new_len, chunk), lambda i, s: (0, 0, 0, i)),
                pl.BlockSpec((2, states.shape[1], chunk), lambda i, s: (0, 0, i)),
                pl.BlockSpec((taps, chunk), lambda i, s: (0, i)),
                pl.BlockSpec((1, chunk), lambda i, s: (0, i)),
                pl.BlockSpec((chunk, cols), lambda i, s: (i, 0)),
            ],
            out_specs=[
                pl.BlockSpec((2, new_len, chunk), lambda i, s: (0, 0, i)),
                pl.BlockSpec((2, new_len, cols), lambda i, s: (0, 0, 0)),
            ],
            scratch_shapes=[pltpu.VMEM((2, 8 + new_len, chunk), jnp.float32)],
        ),
        out_shape=[
            jax.ShapeDtypeStruct((2, new_len, channels), jnp.float32),
            jax.ShapeDtypeStruct((2, new_len, cols), jnp.float32),
        ],
        name="signal",
    )(reading, x, states, w, b, wbc)


def scan_kernel(
    read_ref, bc_ref, sig_ref, dt_ref, z_ref, bias_ref, alog_ref, gain_ref, state_ref,
    out_ref, spread, step_buf, push_buf, scan_buf
):
    states, chunk = alog_ref.shape
    new_len = sig_ref.shape[1]

    @pl.when(pl.program_id(0) == 0)
    def _():
        for r in range(2):
            columns = bc_ref[r].T
            for t in range(new_len):
                spread[r, t] = jnp.broadcast_to(columns[:, t : t + 1], spread.shape[2:])

    decay = -jnp.exp(alog_ref[...])
    hidden = []
    for r in range(2):
        x = dt_ref[r].astype(jnp.float32) + bias_ref[...]
        step = jnp.maximum(x, 0.0) + jnp.log1p(jnp.exp(-jnp.abs(x)))
        step_buf[r] = step
        push_buf[r] = step * sig_ref[r]
    hidden = (
        jnp.where(read_ref[0] > 0, state_ref[0, :states].astype(jnp.float32), 0.0),
        state_ref[1, :states].astype(jnp.float32),
    )
    tiles = chunk // HD
    for t in range(new_len):
        state = []
        for r in range(2):
            now = jnp.broadcast_to(step_buf[r, t : t + 1], (states, chunk))
            push = jnp.broadcast_to(push_buf[r, t : t + 1], (states, chunk))
            both = spread[r, t]
            gain = jnp.concatenate([both[:states]] * tiles, axis=1)
            read = jnp.concatenate([both[states:]] * tiles, axis=1)
            new = jnp.exp(now * decay) * hidden[r] + gain * push
            scan_buf[r, t : t + 1] = jnp.sum(read * new, axis=0, keepdims=True)
            state.append(new)
        hidden = tuple(state)
    for r in range(2):
        z = z_ref[r].astype(jnp.float32)
        full = scan_buf[r] + gain_ref[...] * sig_ref[r]
        out_ref[r] = (full * (z * jax.nn.sigmoid(z))).astype(out_ref.dtype)


def scan_call(reading, bc, signal, dt, z, bias, alog, gain, packed):
    _, new_len, channels = signal.shape
    states, cols = alog.shape[0], bc.shape[2]
    chunk = CHUNK
    row = pl.BlockSpec((1, chunk), lambda i, s: (0, i))
    state = pl.BlockSpec((states, chunk), lambda i, s: (0, i))
    seq = pl.BlockSpec((None, 2, new_len, chunk), lambda i, s: (0, 0, 0, i))
    return pl.pallas_call(
        scan_kernel,
        grid_spec=pltpu.PrefetchScalarGridSpec(
            num_scalar_prefetch=1,
            grid=(channels // chunk,),
            in_specs=[
                pl.BlockSpec((2, new_len, cols), lambda i, s: (0, 0, 0)),
                pl.BlockSpec((2, new_len, chunk), lambda i, s: (0, 0, i)),
                seq,
                seq,
                row,
                state,
                row,
                pl.BlockSpec((2, packed.shape[1], chunk), lambda i, s: (0, 0, i)),
            ],
            out_specs=pl.BlockSpec((None, 2, new_len, chunk), lambda i, s: (0, 0, 0, i)),
            scratch_shapes=[
                pltpu.VMEM((2, new_len, cols, HD), jnp.float32),
                pltpu.VMEM((2, new_len, chunk), jnp.float32),
                pltpu.VMEM((2, new_len, chunk), jnp.float32),
                pltpu.VMEM((2, new_len, chunk), jnp.float32),
            ],
        ),
        out_shape=jax.ShapeDtypeStruct((1, 2, new_len, channels), jnp.bfloat16),
        name="scan",
    )(reading, bc, signal, dt, z, bias, alog, gain, packed)


def exchange_kernel(
    n, early, owner_ref, holder_ref, prefix_ref, state_ref, send_ref, shared_ref, states_ref, got_ref,
    state_cand, prefix_cand, state_send, prefix_send, sends, recvs, local_sems
):
    me = lax.axis_index("replica")
    rows = prefix_ref.shape[0] // n
    cols = state_ref.shape[2] // n
    barrier = pltpu.get_barrier_semaphore()
    for s in range(1, n):
        pl.semaphore_signal(
            barrier, inc=1, device_id={"replica": lax.rem(me + s, n)}, device_id_type=pl.DeviceIdType.MESH
        )

    def row_piece(k):
        return pl.ds(pl.multiple_of(k * rows, rows), rows)

    def col_piece(k):
        return pl.ds(pl.multiple_of(k * cols, HD), cols)

    def remote(kind, s, source, target):
        return pltpu.make_async_remote_copy(
            src_ref=source,
            dst_ref=target,
            send_sem=sends.at[kind, s],
            recv_sem=recvs.at[kind, s],
            device_id={"replica": lax.rem(me + s, n)},
            device_id_type=pl.DeviceIdType.MESH,
        )

    own_state = pltpu.make_async_copy(
        state_ref.at[:, :, col_piece(me)], state_cand.at[me], local_sems.at[0]
    )
    own_prefix = pltpu.make_async_copy(
        prefix_ref.at[row_piece(me)], prefix_cand.at[me], local_sems.at[1]
    )
    own_block = pltpu.make_async_copy(send_ref.at[me], got_ref.at[me], local_sems.at[2])
    own_state.start()
    own_prefix.start()
    own_block.start()
    pl.semaphore_wait(barrier, n - 1)

    first_state, first_prefix, blocks, second_state, second_prefix = [], [], [], [], []
    for s in range(1, n):
        peer = lax.rem(me + s, n)
        copy = remote(0, s, state_ref.at[:, :, col_piece(peer)], state_cand.at[me])
        copy.start()
        first_state.append(copy)
    for s in range(1, n):
        peer = lax.rem(me + s, n)
        copy = remote(1, s, prefix_ref.at[row_piece(peer)], prefix_cand.at[me])
        copy.start()
        first_prefix.append(copy)

    def send_block(s):
        peer = lax.rem(me + s, n)
        copy = remote(2, s, send_ref.at[peer], got_ref.at[me])
        copy.start()
        blocks.append(copy)

    own_state.wait()
    for copy in first_state:
        copy.wait()
    owner = owner_ref[0]
    for d in range(n):
        state_send[d, 0] = state_cand[owner, 0]
        state_send[d, 1] = state_cand[holder_ref[d], 1]
    for s in range(1, early):
        send_block(s)
    for s in range(1, n):
        peer = lax.rem(me + s, n)
        copy = remote(3, s, state_send.at[peer], states_ref.at[:, :, col_piece(me)])
        copy.start()
        second_state.append(copy)
    mine_state = pltpu.make_async_copy(
        state_send.at[me], states_ref.at[:, :, col_piece(me)], local_sems.at[3]
    )
    mine_state.start()
    own_prefix.wait()
    for copy in first_prefix:
        copy.wait()
    prefix_send[...] = prefix_cand[owner]
    for s in range(1, n):
        copy = remote(4, s, prefix_send, shared_ref.at[row_piece(me)])
        copy.start()
        second_prefix.append(copy)
    mine_prefix = pltpu.make_async_copy(prefix_send, shared_ref.at[row_piece(me)], local_sems.at[4])
    mine_prefix.start()
    for s in range(early, n):
        send_block(s)
    own_block.wait()
    mine_state.wait()
    mine_prefix.wait()
    for copy in second_state + second_prefix + blocks:
        copy.wait()


def exchange(owner_id, state_src, prefix, states, send_kv):
    n = send_kv.shape[0]
    any_spec = pl.BlockSpec(memory_space=pl.ANY)
    smem = pl.BlockSpec(memory_space=pltpu.SMEM)
    rows, cols = prefix.shape[0] // n, states.shape[2] // n
    two, height = states.shape[:2]
    early = 1 + n // 4
    return pl.pallas_call(
        lambda *refs: exchange_kernel(n, early, *refs),
        in_specs=[smem, smem, any_spec, any_spec, any_spec],
        out_specs=[any_spec] * 3,
        out_shape=[
            jax.ShapeDtypeStruct(prefix.shape, prefix.dtype),
            jax.ShapeDtypeStruct(states.shape, states.dtype),
            jax.ShapeDtypeStruct(send_kv.shape, send_kv.dtype),
        ],
        scratch_shapes=[
            pltpu.VMEM((n, two, height, cols), states.dtype),
            pltpu.VMEM((n, rows, prefix.shape[1]), prefix.dtype),
            pltpu.VMEM((n, two, height, cols), states.dtype),
            pltpu.VMEM((rows, prefix.shape[1]), prefix.dtype),
            pltpu.SemaphoreType.DMA((5, n)),
            pltpu.SemaphoreType.DMA((5, n)),
            pltpu.SemaphoreType.DMA((5,)),
        ],
        compiler_params=pltpu.CompilerParams(collective_id=0, has_side_effects=True),
        name="exchange",
    )(owner_id, state_src, prefix, states, send_kv)


def local(
    queries,
    new_kv,
    cached_lookup_pairs,
    prefix_ssm,
    prefix_conv,
    pool_kv,
    pool_ssm,
    pool_conv,
    owner_id,
    readers,
    restore_src,
    restore_blk,
    state_src,
    ctx_blocks,
    mamba_x,
    mamba_z,
    mamba_dt,
    dt_bias,
    a_log,
    bypass_gain,
    conv_w,
    conv_b,
    w_bc,
):
    block_len = pool_kv.shape[2]
    own_index = lax.axis_index("replica")
    my_sources = lax.dynamic_index_in_dim(restore_src, own_index, 0, keepdims=False)
    picked = jnp.sum(jnp.where(restore_src == own_index, restore_blk, 0), axis=1)
    send_kv = jnp.take(pool_kv[0], picked, axis=0, mode="clip")
    state_dim, taps = prefix_ssm.shape[1], prefix_conv.shape[1]
    pad = -(state_dim + taps) % 8
    states = jnp.stack(
        [
            jnp.pad(jnp.concatenate([ssm[0], conv[0]], axis=0), ((0, pad), (0, 0)))
            for ssm, conv in ((prefix_ssm, prefix_conv), (pool_ssm, pool_conv))
        ]
    )
    prefix, states, got_kv = exchange(owner_id, state_src, cached_lookup_pairs[0], states, send_kv)
    reading = (readers > 0).astype(jnp.int32)
    signal, partial_bc = signal_call(reading, mamba_x, states, conv_w, conv_b[None], w_bc)
    state_bc = lax.psum(partial_bc, "channel")
    mamba_out = scan_call(
        reading, state_bc, signal, mamba_dt, mamba_z, dt_bias[None], a_log, bypass_gain[None], states
    )
    parts = prefix.shape[0] // block_len
    prefix_blocks = prefix.reshape(parts, block_len, prefix.shape[1])
    fresh_out = attend(
        0, queries, prefix_blocks, lax.iota(jnp.int32, parts), reading * prefix.shape[0], new_kv
    )
    resumed_out = attend(1, queries, got_kv, my_sources, ctx_blocks * block_len, new_kv)
    return (jnp.stack([fresh_out, resumed_out])[None], mamba_out)


def placed_specs():
    return (
        P(("groups", "replica"), None, None, "channel"),
        P(("groups", "replica"), None, None, "channel"),
        P(("groups", "replica"), None, "channel"),
        P(("groups", "replica"), None, "channel"),
        P(("groups", "replica"), None, "channel"),
        P(("groups", "replica"), None, None, "channel"),
        P(("groups", "replica"), None, "channel"),
        P(("groups", "replica"), None, "channel"),
        P("groups"),
        P(("groups", "replica")),
        P("groups", None),
        P("groups", None),
        P("groups"),
        P(("groups", "replica")),
        P(("groups", "replica"), None, None, "channel"),
        P(("groups", "replica"), None, None, "channel"),
        P(("groups", "replica"), None, None, "channel"),
        P("channel"),
        P(None, "channel"),
        P("channel"),
        P(None, "channel"),
        P("channel"),
        P("channel", None),
    )


def solution(mesh):
    return jax.shard_map(
        local,
        mesh=mesh,
        in_specs=placed_specs(),
        out_specs=(
            P(("groups", "replica"), None, None, "channel"),
            P(("groups", "replica"), None, None, "channel"),
        ),
        check_vma=False,
    )
```

```python
import jax
import jax.numpy as jnp
from jax import lax
from jax.experimental import pallas as pl
from jax.experimental.pallas import tpu as pltpu
from jax.sharding import PartitionSpec as P

HD = 128
Q_PER_KV = 8
CHUNKS = 4


def attend_kernel(parts, src_ref, live_ref, q_ref, *refs):
    ctx_refs, new_ref, out_ref = refs[:parts], refs[parts], refs[parts + 1]
    new_len = q_ref.shape[0]
    heads = new_ref.shape[1] // (2 * HD)
    factor = HD ** (-0.5)
    rows = Q_PER_KV * new_len
    live = live_ref[0]
    for head in range(heads):
        query = jnp.concatenate(
            [
                q_ref[:, (head * Q_PER_KV + g) * HD : (head * Q_PER_KV + g + 1) * HD]
                for g in range(Q_PER_KV)
            ],
            axis=0,
        )
        key_cols = slice(2 * head * HD, (2 * head + 1) * HD)
        value_cols = slice((2 * head + 1) * HD, (2 * head + 2) * HD)
        contract = (((1,), (1,)), ((), ()))
        scores = []
        start = 0
        for ref in ctx_refs:
            piece = (
                lax.dot_general(
                    query, ref[:, key_cols], contract, preferred_element_type=jnp.float32
                )
                * factor
            )
            position = start + lax.broadcasted_iota(jnp.int32, piece.shape, 1)
            scores.append(jnp.where(position < live, piece, -jnp.inf))
            start += ref.shape[0]
        fresh = (
            lax.dot_general(
                query, new_ref[:, key_cols], contract, preferred_element_type=jnp.float32
            )
            * factor
        )
        time = lax.rem(lax.broadcasted_iota(jnp.int32, fresh.shape, 0), new_len)
        fresh = jnp.where(
            time >= lax.broadcasted_iota(jnp.int32, fresh.shape, 1), fresh, -jnp.inf
        )
        highest = jnp.max(fresh, axis=1, keepdims=True)
        for piece in scores:
            highest = jnp.maximum(highest, jnp.max(piece, axis=1, keepdims=True))
        weight = jnp.exp(fresh - highest)
        total = jnp.sum(weight, axis=1, keepdims=True)
        mixed = jnp.dot(
            weight.astype(jnp.bfloat16),
            new_ref[:, value_cols],
            preferred_element_type=jnp.float32,
        )
        for piece, ref in zip(scores, ctx_refs):
            weight = jnp.exp(piece - highest)
            total = total + jnp.sum(weight, axis=1, keepdims=True)
            mixed = mixed + jnp.dot(
                weight.astype(jnp.bfloat16),
                ref[:, value_cols],
                preferred_element_type=jnp.float32,
            )
        result = (mixed / total).astype(out_ref.dtype)
        for g in range(Q_PER_KV):
            at = (head * Q_PER_KV + g) * HD
            out_ref[:, at : at + HD] = result[g * new_len : (g + 1) * new_len]


def attend(request, queries, blocks, block_len, source, live, new_kv):
    parts = source.shape[0]
    width = blocks.shape[1]
    _, _, new_len, q_width = queries.shape

    def pick(j):
        return pl.BlockSpec((block_len, width), lambda i, s, l: (s[j], 0))

    return pl.pallas_call(
        lambda *refs: attend_kernel(parts, *refs),
        grid_spec=pltpu.PrefetchScalarGridSpec(
            num_scalar_prefetch=2,
            grid=(1,),
            in_specs=[
                pl.BlockSpec((None, None, new_len, q_width), lambda i, s, l: (0, request, 0, 0))
            ]
            + [pick(j) for j in range(parts)]
            + [pl.BlockSpec((None, None, new_len, width), lambda i, s, l: (0, request, 0, 0))],
            out_specs=pl.BlockSpec((new_len, q_width), lambda i, s, l: (0, 0)),
        ),
        out_shape=jax.ShapeDtypeStruct((new_len, q_width), jnp.bfloat16),
        name="attend",
    )(source, live, queries, *([blocks] * parts), new_kv)


def signal_kernel(read_ref, x_ref, shared_ref, pool_ref, w_ref, b_ref, wbc_ref, sig_ref, bc_ref, pad):
    taps = w_ref.shape[0]
    new_len = x_ref.shape[1]
    reading = read_ref[0] > 0
    base = 8 - (taps - 1)
    start = wbc_ref.shape[1] // 2
    shared = shared_ref[...].astype(jnp.float32)[start : start + taps - 1]
    pad[0, base:8] = jnp.where(reading, shared, 0.0)
    pad[1, base:8] = pool_ref[...].astype(jnp.float32)[start : start + taps - 1]

    @pl.when(pl.program_id(0) == 0)
    def _():
        bc_ref[...] = jnp.zeros_like(bc_ref)

    for r in range(2):
        pad[r, 8 : 8 + new_len] = x_ref[r].astype(jnp.float32)
        total = b_ref[...] + w_ref[0:1] * pad[r, base : base + new_len]
        for k in range(1, taps):
            total = total + w_ref[k : k + 1] * pad[r, base + k : base + k + new_len]
        signal = total * jax.nn.sigmoid(total)
        sig_ref[r] = signal
        bc_ref[r] += jnp.dot(
            signal.astype(jnp.bfloat16), wbc_ref[...], preferred_element_type=jnp.float32
        )


def signal_call(reading, x, shared, offset, pool, w, b, wbc):
    _, _, new_len, channels = x.shape
    taps, cols = w.shape[0], wbc.shape[1]
    chunk = pool.shape[2]
    return pl.pallas_call(
        signal_kernel,
        grid_spec=pltpu.PrefetchScalarGridSpec(
            num_scalar_prefetch=1,
            grid=(channels // chunk,),
            in_specs=[
                pl.BlockSpec((None, 2, new_len, chunk), lambda i, s: (0, 0, 0, i)),
                pl.BlockSpec((None, shared.shape[1], chunk), lambda i, s: (offset + i, 0, 0)),
                pl.BlockSpec((None, pool.shape[1], chunk), lambda i, s: (i, 0, 0)),
                pl.BlockSpec((taps, chunk), lambda i, s: (0, i)),
                pl.BlockSpec((1, chunk), lambda i, s: (0, i)),
                pl.BlockSpec((chunk, cols), lambda i, s: (i, 0)),
            ],
            out_specs=[
                pl.BlockSpec((2, new_len, chunk), lambda i, s: (0, 0, i)),
                pl.BlockSpec((2, new_len, cols), lambda i, s: (0, 0, 0)),
            ],
            scratch_shapes=[pltpu.VMEM((2, 8 + new_len, chunk), jnp.float32)],
        ),
        out_shape=[
            jax.ShapeDtypeStruct((2, new_len, channels), jnp.float32),
            jax.ShapeDtypeStruct((2, new_len, cols), jnp.float32),
        ],
        name="signal",
    )(reading, x, shared, pool, w, b, wbc)


def scan_kernel(
    read_ref, bc_ref, sig_ref, dt_ref, z_ref, bias_ref, alog_ref, gain_ref, shared_ref, pool_ref,
    out_ref, spread, step_buf, push_buf, scan_buf
):
    states, chunk = alog_ref.shape
    new_len = sig_ref.shape[1]

    @pl.when(pl.program_id(0) == 0)
    def _():
        for r in range(2):
            columns = bc_ref[r].T
            for t in range(new_len):
                spread[r, t] = jnp.broadcast_to(columns[:, t : t + 1], spread.shape[2:])

    decay = -jnp.exp(alog_ref[...])
    hidden = []
    for r in range(2):
        x = dt_ref[r].astype(jnp.float32) + bias_ref[...]
        step = jnp.maximum(x, 0.0) + jnp.log1p(jnp.exp(-jnp.abs(x)))
        step_buf[r] = step
        push_buf[r] = step * sig_ref[r]
    hidden = (
        jnp.where(read_ref[0] > 0, shared_ref[...].astype(jnp.float32)[:states], 0.0),
        pool_ref[...].astype(jnp.float32)[:states],
    )
    tiles = chunk // HD
    for t in range(new_len):
        state = []
        for r in range(2):
            now = jnp.broadcast_to(step_buf[r, t : t + 1], (states, chunk))
            push = jnp.broadcast_to(push_buf[r, t : t + 1], (states, chunk))
            both = spread[r, t]
            gain = jnp.concatenate([both[:states]] * tiles, axis=1)
            read = jnp.concatenate([both[states:]] * tiles, axis=1)
            new = jnp.exp(now * decay) * hidden[r] + gain * push
            scan_buf[r, t : t + 1] = jnp.sum(read * new, axis=0, keepdims=True)
            state.append(new)
        hidden = tuple(state)
    for r in range(2):
        z = z_ref[r].astype(jnp.float32)
        full = scan_buf[r] + gain_ref[...] * sig_ref[r]
        out_ref[r] = (full * (z * jax.nn.sigmoid(z))).astype(out_ref.dtype)


def scan_call(reading, bc, signal, dt, z, bias, alog, gain, shared, offset, pool):
    _, new_len, channels = signal.shape
    states, cols = alog.shape[0], bc.shape[2]
    chunk = pool.shape[2]
    row = pl.BlockSpec((1, chunk), lambda i, s: (0, i))
    state = pl.BlockSpec((states, chunk), lambda i, s: (0, i))
    seq = pl.BlockSpec((None, 2, new_len, chunk), lambda i, s: (0, 0, 0, i))
    return pl.pallas_call(
        scan_kernel,
        grid_spec=pltpu.PrefetchScalarGridSpec(
            num_scalar_prefetch=1,
            grid=(channels // chunk,),
            in_specs=[
                pl.BlockSpec((2, new_len, cols), lambda i, s: (0, 0, 0)),
                pl.BlockSpec((2, new_len, chunk), lambda i, s: (0, 0, i)),
                seq,
                seq,
                row,
                state,
                row,
                pl.BlockSpec((None, shared.shape[1], chunk), lambda i, s: (offset + i, 0, 0)),
                pl.BlockSpec((None, pool.shape[1], chunk), lambda i, s: (i, 0, 0)),
            ],
            out_specs=pl.BlockSpec((None, 2, new_len, chunk), lambda i, s: (0, 0, 0, i)),
            scratch_shapes=[
                pltpu.VMEM((2, new_len, cols, HD), jnp.float32),
                pltpu.VMEM((2, new_len, chunk), jnp.float32),
                pltpu.VMEM((2, new_len, chunk), jnp.float32),
                pltpu.VMEM((2, new_len, chunk), jnp.float32),
            ],
        ),
        out_shape=jax.ShapeDtypeStruct((1, 2, new_len, channels), jnp.bfloat16),
        name="scan",
    )(reading, bc, signal, dt, z, bias, alog, gain, shared, pool)


def exchange_kernel(
    n, owner_ref, holder_ref, prefix_ref, state_ref, send_ref, shared_ref, states_ref, got_ref,
    state_cand, state_send, own, side, rightward, leftward, to_right, to_left, final,
    sends, recvs, chain_sends, chain_recvs, local_sems
):
    me = lax.axis_index("replica")
    chunks = prefix_ref.shape[1]
    line, half = me // 2, lax.rem(me, 2)
    length = n // 2
    last = length - 1
    partner = line * 2 + 1 - half
    owner = owner_ref[0]
    owner_line = owner // 2
    barrier = pltpu.get_barrier_semaphore()
    for s in range(1, n):
        pl.semaphore_signal(
            barrier, inc=1, device_id={"replica": lax.rem(me + s, n)}, device_id_type=pl.DeviceIdType.MESH
        )

    def remote(source, target, send_sem, recv_sem, peer):
        return pltpu.make_async_remote_copy(
            src_ref=source,
            dst_ref=target,
            send_sem=send_sem,
            recv_sem=recv_sem,
            device_id={"replica": peer},
            device_id_type=pl.DeviceIdType.MESH,
        )

    def spread(kind, s, source, target):
        return remote(
            source, target, sends.at[kind, s], recvs.at[kind, s], lax.rem(me + s, n)
        )

    def chain(kind, c, source, target, peer):
        return remote(source, target, chain_sends.at[kind, c], chain_recvs.at[kind, c], peer)

    own_prefix = pltpu.make_async_copy(prefix_ref.at[half], own, local_sems.at[0])
    own_state = pltpu.make_async_copy(state_ref.at[me], state_cand.at[me], local_sems.at[1])
    own_block = pltpu.make_async_copy(send_ref.at[me], got_ref.at[me], local_sems.at[2])
    own_prefix.start()
    own_state.start()
    own_block.start()
    pl.semaphore_wait(barrier, n - 1)

    first_state, blocks, second_state, sideways = [], [], [], []
    for s in range(1, n):
        copy = spread(0, s, state_ref.at[lax.rem(me + s, n)], state_cand.at[me])
        copy.start()
        first_state.append(copy)
    for c in range(chunks):
        copy = chain(0, c, prefix_ref.at[1 - half, c], side.at[c], partner)
        copy.start()
        sideways.append(copy)

    def send_block(s):
        copy = spread(1, s, send_ref.at[lax.rem(me + s, n)], got_ref.at[me])
        copy.start()
        blocks.append(copy)

    send_block(1)
    own_state.wait()
    for copy in first_state:
        copy.wait()
    for d in range(n):
        state_send[d] = state_cand[holder_ref[d]]
    for s in range(1, n):
        copy = spread(2, s, state_send.at[lax.rem(me + s, n)], states_ref.at[me])
        copy.start()
        second_state.append(copy)
    mine_state = pltpu.make_async_copy(state_send.at[me], states_ref.at[me], local_sems.at[3])
    mine_state.start()
    own_prefix.wait()

    def right_copy(c):
        return chain(1, c, to_right.at[c], rightward.at[c], lax.rem(me + 2, n))

    def left_copy(c):
        return chain(2, c, to_left.at[c], leftward.at[c], lax.rem(me + n - 2, n))

    def final_copy(c):
        return chain(3, c, final.at[c], shared_ref.at[half, c], partner)

    def keep_copy(c):
        return pltpu.make_async_copy(final.at[c], shared_ref.at[half, c], local_sems.at[4 + c])

    def here(c):
        return jnp.where(owner == me, own[c], side[c])

    near, far = jnp.minimum(line, last - line), jnp.maximum(line, last - line)
    steps = chunks + length - 1
    sent = 2
    for t in range(steps):
        c_near, c_right, c_left, c_far = t - near, t - line, t - (last - line), t - far

        @pl.when((c_near >= 0) & (c_near < chunks))
        def _():
            chain(0, c_near, side.at[c_near], side.at[c_near], partner).wait_recv()

        @pl.when((c_right >= 0) & (c_right < chunks))
        def _():
            @pl.when(line > 0)
            def _():
                right_copy(c_right).wait_recv()

            @pl.when(line < last)
            def _():
                to_right[c_right] = jnp.where(
                    owner_line == line, here(c_right), rightward[c_right]
                )
                right_copy(c_right).start()

        @pl.when((c_left >= 0) & (c_left < chunks))
        def _():
            @pl.when(line < last)
            def _():
                left_copy(c_left).wait_recv()

            @pl.when(line > 0)
            def _():
                to_left[c_left] = jnp.where(owner_line == line, here(c_left), leftward[c_left])
                left_copy(c_left).start()

        @pl.when((c_far >= 0) & (c_far < chunks))
        def _():
            final[c_far] = jnp.where(
                owner_line == line,
                here(c_far),
                jnp.where(owner_line < line, rightward[c_far], leftward[c_far]),
            )
            final_copy(c_far).start()
            keep_copy(c_far).start()

        upto = 2 + ((n - 2) * (t + 1)) // steps
        while sent < upto:
            send_block(sent)
            sent += 1
    for s in range(sent, n):
        send_block(s)
    own_block.wait()
    mine_state.wait()
    for copy in sideways:
        copy.wait_send()
    for c in range(chunks):
        keep_copy(c).wait()
        final_copy(c).wait()

        @pl.when(line < last)
        def _():
            right_copy(c).wait_send()

        @pl.when(line > 0)
        def _():
            left_copy(c).wait_send()

    for copy in second_state + blocks:
        copy.wait()


def exchange(owner_id, state_src, prefix, states, send_kv):
    n = send_kv.shape[0]
    any_spec = pl.BlockSpec(memory_space=pl.ANY)
    smem = pl.BlockSpec(memory_space=pltpu.SMEM)
    piece = pltpu.VMEM(prefix.shape[1:], prefix.dtype)
    chunks = prefix.shape[1]
    return pl.pallas_call(
        lambda *refs: exchange_kernel(n, *refs),
        in_specs=[smem, smem, any_spec, any_spec, any_spec],
        out_specs=[any_spec] * 3,
        out_shape=[
            jax.ShapeDtypeStruct(prefix.shape, prefix.dtype),
            jax.ShapeDtypeStruct(states.shape, states.dtype),
            jax.ShapeDtypeStruct(send_kv.shape, send_kv.dtype),
        ],
        scratch_shapes=[
            pltpu.VMEM(states.shape, states.dtype),
            pltpu.VMEM(states.shape, states.dtype),
        ]
        + [piece] * 7
        + [
            pltpu.SemaphoreType.DMA((3, n)),
            pltpu.SemaphoreType.DMA((3, n)),
            pltpu.SemaphoreType.DMA((4, chunks)),
            pltpu.SemaphoreType.DMA((4, chunks)),
            pltpu.SemaphoreType.DMA((4 + chunks,)),
        ],
        compiler_params=pltpu.CompilerParams(collective_id=0, has_side_effects=True),
        name="exchange",
    )(owner_id, state_src, prefix, states, send_kv)


def pack_states(ssm, conv, unit, width):
    rows = ssm.shape[0] + conv.shape[0]
    joined = jnp.pad(jnp.concatenate([ssm, conv], axis=0), ((0, -rows % unit), (0, 0)))
    return jnp.swapaxes(joined.reshape(joined.shape[0], -1, width), 0, 1)


def local(
    queries,
    new_kv,
    cached_lookup_pairs,
    prefix_ssm,
    prefix_conv,
    pool_kv,
    pool_ssm,
    pool_conv,
    owner_id,
    readers,
    restore_src,
    restore_blk,
    state_src,
    ctx_blocks,
    mamba_x,
    mamba_z,
    mamba_dt,
    dt_bias,
    a_log,
    bypass_gain,
    conv_w,
    conv_b,
    w_bc,
):
    block_len = pool_kv.shape[2]
    own_index = lax.axis_index("replica")
    my_sources = lax.dynamic_index_in_dim(restore_src, own_index, 0, keepdims=False)
    picked = jnp.sum(jnp.where(restore_src == own_index, restore_blk, 0), axis=1)
    send_kv = jnp.take(pool_kv[0], picked, axis=0, mode="clip")
    n, width, channels = restore_src.shape[0], cached_lookup_pairs.shape[2], pool_ssm.shape[2]
    length = cached_lookup_pairs.shape[1]
    pool_states = pack_states(pool_ssm[0], pool_conv[0], 8, channels // n)
    prefix_states = pack_states(prefix_ssm[0], prefix_conv[0], 16, width)
    groups, height = prefix_states.shape[:2]
    packed = jnp.concatenate([cached_lookup_pairs[0], prefix_states.reshape(-1, width)], axis=0)
    shared, pool_states, got_kv = exchange(
        owner_id, state_src, packed.reshape(2, CHUNKS, -1, width), pool_states, send_kv
    )
    shared = shared.reshape(packed.shape)
    if groups == n:
        offset = length // height
        prefix_states = shared.reshape(-1, height, width)
    else:
        offset = 0
        prefix_states = shared[length:].reshape(groups, height, width)
        prefix_states = jnp.swapaxes(prefix_states, 0, 1).reshape(height, n, channels // n)
        prefix_states = jnp.swapaxes(prefix_states, 0, 1)
    reading = (readers > 0).astype(jnp.int32)
    signal, partial_bc = signal_call(
        reading, mamba_x, prefix_states, offset, pool_states, conv_w, conv_b[None], w_bc
    )
    state_bc = lax.psum(partial_bc, "channel")
    mamba_out = scan_call(
        reading, state_bc, signal, mamba_dt, mamba_z, dt_bias[None], a_log, bypass_gain[None],
        prefix_states, offset, pool_states
    )
    parts = length // block_len
    fresh_out = attend(
        0, queries, shared, block_len, lax.iota(jnp.int32, parts), reading * length, new_kv
    )
    resumed_out = attend(
        1, queries, got_kv.reshape(-1, width), block_len, my_sources, ctx_blocks * block_len, new_kv
    )
    return (jnp.stack([fresh_out, resumed_out])[None], mamba_out)


def placed_specs():
    return (
        P(("groups", "replica"), None, None, "channel"),
        P(("groups", "replica"), None, None, "channel"),
        P(("groups", "replica"), None, "channel"),
        P(("groups", "replica"), None, "channel"),
        P(("groups", "replica"), None, "channel"),
        P(("groups", "replica"), None, None, "channel"),
        P(("groups", "replica"), None, "channel"),
        P(("groups", "replica"), None, "channel"),
        P("groups"),
        P(("groups", "replica")),
        P("groups", None),
        P("groups", None),
        P("groups"),
        P(("groups", "replica")),
        P(("groups", "replica"), None, None, "channel"),
        P(("groups", "replica"), None, None, "channel"),
        P(("groups", "replica"), None, None, "channel"),
        P("channel"),
        P(None, "channel"),
        P("channel"),
        P(None, "channel"),
        P("channel"),
        P("channel", None),
    )


def solution(mesh):
    return jax.shard_map(
        local,
        mesh=mesh,
        in_specs=placed_specs(),
        out_specs=(
            P(("groups", "replica"), None, None, "channel"),
            P(("groups", "replica"), None, None, "channel"),
        ),
        check_vma=False,
    )
```

```python
import jax
import jax.numpy as jnp
from jax import lax
from jax.experimental import pallas as pl
from jax.experimental.pallas import tpu as pltpu
from jax.sharding import PartitionSpec as P

HD = 128
Q_PER_KV = 8
CHUNKS = 4


def attend_kernel(parts, src_ref, live_ref, q_ref, *refs):
    ctx_refs, new_ref, out_ref = refs[:parts], refs[parts], refs[parts + 1]
    new_len = q_ref.shape[0]
    heads = new_ref.shape[1] // (2 * HD)
    factor = HD ** (-0.5)
    rows = Q_PER_KV * new_len
    live = live_ref[0]
    for head in range(heads):
        query = jnp.concatenate(
            [
                q_ref[:, (head * Q_PER_KV + g) * HD : (head * Q_PER_KV + g + 1) * HD]
                for g in range(Q_PER_KV)
            ],
            axis=0,
        )
        key_cols = slice(2 * head * HD, (2 * head + 1) * HD)
        value_cols = slice((2 * head + 1) * HD, (2 * head + 2) * HD)
        contract = (((1,), (1,)), ((), ()))
        scores = []
        start = 0
        for ref in ctx_refs:
            piece = (
                lax.dot_general(
                    query, ref[:, key_cols], contract, preferred_element_type=jnp.float32
                )
                * factor
            )
            position = start + lax.broadcasted_iota(jnp.int32, piece.shape, 1)
            scores.append(jnp.where(position < live, piece, -jnp.inf))
            start += ref.shape[0]
        fresh = (
            lax.dot_general(
                query, new_ref[:, key_cols], contract, preferred_element_type=jnp.float32
            )
            * factor
        )
        time = lax.rem(lax.broadcasted_iota(jnp.int32, fresh.shape, 0), new_len)
        fresh = jnp.where(
            time >= lax.broadcasted_iota(jnp.int32, fresh.shape, 1), fresh, -jnp.inf
        )
        highest = jnp.max(fresh, axis=1, keepdims=True)
        for piece in scores:
            highest = jnp.maximum(highest, jnp.max(piece, axis=1, keepdims=True))
        weight = jnp.exp(fresh - highest)
        total = jnp.sum(weight, axis=1, keepdims=True)
        mixed = jnp.dot(
            weight.astype(jnp.bfloat16),
            new_ref[:, value_cols],
            preferred_element_type=jnp.float32,
        )
        for piece, ref in zip(scores, ctx_refs):
            weight = jnp.exp(piece - highest)
            total = total + jnp.sum(weight, axis=1, keepdims=True)
            mixed = mixed + jnp.dot(
                weight.astype(jnp.bfloat16),
                ref[:, value_cols],
                preferred_element_type=jnp.float32,
            )
        result = (mixed / total).astype(out_ref.dtype)
        for g in range(Q_PER_KV):
            at = (head * Q_PER_KV + g) * HD
            out_ref[:, at : at + HD] = result[g * new_len : (g + 1) * new_len]


def attend(request, queries, blocks, block_len, source, live, new_kv):
    parts = source.shape[0]
    width = blocks.shape[1]
    _, _, new_len, q_width = queries.shape

    def pick(j):
        return pl.BlockSpec((block_len, width), lambda i, s, l: (s[j], 0))

    return pl.pallas_call(
        lambda *refs: attend_kernel(parts, *refs),
        grid_spec=pltpu.PrefetchScalarGridSpec(
            num_scalar_prefetch=2,
            grid=(1,),
            in_specs=[
                pl.BlockSpec((None, None, new_len, q_width), lambda i, s, l: (0, request, 0, 0))
            ]
            + [pick(j) for j in range(parts)]
            + [pl.BlockSpec((None, None, new_len, width), lambda i, s, l: (0, request, 0, 0))],
            out_specs=pl.BlockSpec((new_len, q_width), lambda i, s, l: (0, 0)),
        ),
        out_shape=jax.ShapeDtypeStruct((new_len, q_width), jnp.bfloat16),
        name="attend",
    )(source, live, queries, *([blocks] * parts), new_kv)


def signal_kernel(read_ref, x_ref, shared_ref, pool_ref, w_ref, b_ref, wbc_ref, sig_ref, bc_ref, pad):
    taps = w_ref.shape[0]
    new_len = x_ref.shape[1]
    reading = read_ref[0] > 0
    base = 8 - (taps - 1)
    start = wbc_ref.shape[1] // 2
    shared = shared_ref[...].astype(jnp.float32)[start : start + taps - 1]
    pad[0, base:8] = jnp.where(reading, shared, 0.0)
    pad[1, base:8] = pool_ref[...].astype(jnp.float32)[start : start + taps - 1]

    @pl.when(pl.program_id(0) == 0)
    def _():
        bc_ref[...] = jnp.zeros_like(bc_ref)

    for r in range(2):
        pad[r, 8 : 8 + new_len] = x_ref[r].astype(jnp.float32)
        total = b_ref[...] + w_ref[0:1] * pad[r, base : base + new_len]
        for k in range(1, taps):
            total = total + w_ref[k : k + 1] * pad[r, base + k : base + k + new_len]
        signal = total * jax.nn.sigmoid(total)
        sig_ref[r] = signal
        bc_ref[r] += jnp.dot(
            signal.astype(jnp.bfloat16), wbc_ref[...], preferred_element_type=jnp.float32
        )


def signal_call(reading, x, shared, offset, pool, w, b, wbc):
    _, _, new_len, channels = x.shape
    taps, cols = w.shape[0], wbc.shape[1]
    chunk = pool.shape[2]
    return pl.pallas_call(
        signal_kernel,
        grid_spec=pltpu.PrefetchScalarGridSpec(
            num_scalar_prefetch=1,
            grid=(channels // chunk,),
            in_specs=[
                pl.BlockSpec((None, 2, new_len, chunk), lambda i, s: (0, 0, 0, i)),
                pl.BlockSpec((None, shared.shape[1], chunk), lambda i, s: (offset + i, 0, 0)),
                pl.BlockSpec((None, pool.shape[1], chunk), lambda i, s: (i, 0, 0)),
                pl.BlockSpec((taps, chunk), lambda i, s: (0, i)),
                pl.BlockSpec((1, chunk), lambda i, s: (0, i)),
                pl.BlockSpec((chunk, cols), lambda i, s: (i, 0)),
            ],
            out_specs=[
                pl.BlockSpec((2, new_len, chunk), lambda i, s: (0, 0, i)),
                pl.BlockSpec((2, new_len, cols), lambda i, s: (0, 0, 0)),
            ],
            scratch_shapes=[pltpu.VMEM((2, 8 + new_len, chunk), jnp.float32)],
        ),
        out_shape=[
            jax.ShapeDtypeStruct((2, new_len, channels), jnp.float32),
            jax.ShapeDtypeStruct((2, new_len, cols), jnp.float32),
        ],
        cost_estimate=pl.CostEstimate(flops=6_000_000_000, bytes_accessed=20_000_000, transcendentals=0),
        name="signal",
    )(reading, x, shared, pool, w, b, wbc)


def scan_kernel(
    read_ref, bc_ref, sig_ref, dt_ref, z_ref, bias_ref, alog_ref, gain_ref, shared_ref, pool_ref,
    out_ref, spread, step_buf, push_buf, scan_buf
):
    states, chunk = alog_ref.shape
    new_len = sig_ref.shape[1]

    @pl.when(pl.program_id(0) == 0)
    def _():
        for r in range(2):
            columns = bc_ref[r].T
            for t in range(new_len):
                spread[r, t] = jnp.broadcast_to(columns[:, t : t + 1], spread.shape[2:])

    decay = -jnp.exp(alog_ref[...])
    hidden = []
    for r in range(2):
        x = dt_ref[r].astype(jnp.float32) + bias_ref[...]
        step = jnp.maximum(x, 0.0) + jnp.log1p(jnp.exp(-jnp.abs(x)))
        step_buf[r] = step
        push_buf[r] = step * sig_ref[r]
    hidden = (
        jnp.where(read_ref[0] > 0, shared_ref[...].astype(jnp.float32)[:states], 0.0),
        pool_ref[...].astype(jnp.float32)[:states],
    )
    tiles = chunk // HD
    for t in range(new_len):
        state = []
        for r in range(2):
            now = jnp.broadcast_to(step_buf[r, t : t + 1], (states, chunk))
            push = jnp.broadcast_to(push_buf[r, t : t + 1], (states, chunk))
            both = spread[r, t]
            gain = jnp.concatenate([both[:states]] * tiles, axis=1)
            read = jnp.concatenate([both[states:]] * tiles, axis=1)
            new = jnp.exp(now * decay) * hidden[r] + gain * push
            scan_buf[r, t : t + 1] = jnp.sum(read * new, axis=0, keepdims=True)
            state.append(new)
        hidden = tuple(state)
    for r in range(2):
        z = z_ref[r].astype(jnp.float32)
        full = scan_buf[r] + gain_ref[...] * sig_ref[r]
        out_ref[r] = (full * (z * jax.nn.sigmoid(z))).astype(out_ref.dtype)


def scan_call(reading, bc, signal, dt, z, bias, alog, gain, shared, offset, pool):
    _, new_len, channels = signal.shape
    states, cols = alog.shape[0], bc.shape[2]
    chunk = pool.shape[2]
    row = pl.BlockSpec((1, chunk), lambda i, s: (0, i))
    state = pl.BlockSpec((states, chunk), lambda i, s: (0, i))
    seq = pl.BlockSpec((None, 2, new_len, chunk), lambda i, s: (0, 0, 0, i))
    return pl.pallas_call(
        scan_kernel,
        grid_spec=pltpu.PrefetchScalarGridSpec(
            num_scalar_prefetch=1,
            grid=(channels // chunk,),
            in_specs=[
                pl.BlockSpec((2, new_len, cols), lambda i, s: (0, 0, 0)),
                pl.BlockSpec((2, new_len, chunk), lambda i, s: (0, 0, i)),
                seq,
                seq,
                row,
                state,
                row,
                pl.BlockSpec((None, shared.shape[1], chunk), lambda i, s: (offset + i, 0, 0)),
                pl.BlockSpec((None, pool.shape[1], chunk), lambda i, s: (i, 0, 0)),
            ],
            out_specs=pl.BlockSpec((None, 2, new_len, chunk), lambda i, s: (0, 0, 0, i)),
            scratch_shapes=[
                pltpu.VMEM((2, new_len, cols, HD), jnp.float32),
                pltpu.VMEM((2, new_len, chunk), jnp.float32),
                pltpu.VMEM((2, new_len, chunk), jnp.float32),
                pltpu.VMEM((2, new_len, chunk), jnp.float32),
            ],
        ),
        out_shape=jax.ShapeDtypeStruct((1, 2, new_len, channels), jnp.bfloat16),
        cost_estimate=pl.CostEstimate(flops=10_000_000_000, bytes_accessed=30_000_000, transcendentals=0),
        name="scan",
    )(reading, bc, signal, dt, z, bias, alog, gain, shared, pool)


def exchange_kernel(
    n, owner_ref, holder_ref, prefix_ref, state_ref, shared_ref, states_ref,
    state_cand, state_send, own, side, rightward, leftward, to_right, to_left, final,
    sends, recvs, chain_sends, chain_recvs, local_sems
):
    me = lax.axis_index("replica")
    chunks = prefix_ref.shape[1]
    line, half = me // 2, lax.rem(me, 2)
    length = n // 2
    last = length - 1
    partner = line * 2 + 1 - half
    owner = owner_ref[0]
    owner_line = owner // 2
    barrier = pltpu.get_barrier_semaphore()
    for s in range(1, n):
        pl.semaphore_signal(
            barrier, inc=1, device_id={"replica": lax.rem(me + s, n)}, device_id_type=pl.DeviceIdType.MESH
        )

    def remote(source, target, send_sem, recv_sem, peer):
        return pltpu.make_async_remote_copy(
            src_ref=source,
            dst_ref=target,
            send_sem=send_sem,
            recv_sem=recv_sem,
            device_id={"replica": peer},
            device_id_type=pl.DeviceIdType.MESH,
        )

    def spread(kind, s, source, target):
        return remote(
            source, target, sends.at[kind, s], recvs.at[kind, s], lax.rem(me + s, n)
        )

    def chain(kind, c, source, target, peer):
        return remote(source, target, chain_sends.at[kind, c], chain_recvs.at[kind, c], peer)

    own_prefix = pltpu.make_async_copy(prefix_ref.at[half], own, local_sems.at[0])
    own_state = pltpu.make_async_copy(state_ref.at[me], state_cand.at[me], local_sems.at[1])
    own_prefix.start()
    own_state.start()
    pl.semaphore_wait(barrier, n - 1)

    first_state, second_state, sideways = [], [], []
    for s in range(1, n):
        copy = spread(0, s, state_ref.at[lax.rem(me + s, n)], state_cand.at[me])
        copy.start()
        first_state.append(copy)
    for c in range(chunks):
        copy = chain(0, c, prefix_ref.at[1 - half, c], side.at[c], partner)
        copy.start()
        sideways.append(copy)

    own_state.wait()
    for copy in first_state:
        copy.wait()
    for d in range(n):
        state_send[d] = state_cand[holder_ref[d]]
    for s in range(1, n):
        copy = spread(2, s, state_send.at[lax.rem(me + s, n)], states_ref.at[me])
        copy.start()
        second_state.append(copy)
    mine_state = pltpu.make_async_copy(state_send.at[me], states_ref.at[me], local_sems.at[3])
    mine_state.start()
    own_prefix.wait()

    def right_copy(c):
        return chain(1, c, to_right.at[c], rightward.at[c], lax.rem(me + 2, n))

    def left_copy(c):
        return chain(2, c, to_left.at[c], leftward.at[c], lax.rem(me + n - 2, n))

    def final_copy(c):
        return chain(3, c, final.at[c], shared_ref.at[half, c], partner)

    def keep_copy(c):
        return pltpu.make_async_copy(final.at[c], shared_ref.at[half, c], local_sems.at[4 + c])

    def here(c):
        return jnp.where(owner == me, own[c], side[c])

    near, far = jnp.minimum(line, last - line), jnp.maximum(line, last - line)
    steps = chunks + length - 1
    for t in range(steps):
        c_near, c_right, c_left, c_far = t - near, t - line, t - (last - line), t - far

        @pl.when((c_near >= 0) & (c_near < chunks))
        def _():
            chain(0, c_near, side.at[c_near], side.at[c_near], partner).wait_recv()

        @pl.when((c_right >= 0) & (c_right < chunks))
        def _():
            @pl.when(line > 0)
            def _():
                right_copy(c_right).wait_recv()

            @pl.when(line < last)
            def _():
                to_right[c_right] = jnp.where(
                    owner_line == line, here(c_right), rightward[c_right]
                )
                right_copy(c_right).start()

        @pl.when((c_left >= 0) & (c_left < chunks))
        def _():
            @pl.when(line < last)
            def _():
                left_copy(c_left).wait_recv()

            @pl.when(line > 0)
            def _():
                to_left[c_left] = jnp.where(owner_line == line, here(c_left), leftward[c_left])
                left_copy(c_left).start()

        @pl.when((c_far >= 0) & (c_far < chunks))
        def _():
            final[c_far] = jnp.where(
                owner_line == line,
                here(c_far),
                jnp.where(owner_line < line, rightward[c_far], leftward[c_far]),
            )
            final_copy(c_far).start()
            keep_copy(c_far).start()

    mine_state.wait()
    for copy in sideways:
        copy.wait_send()
    for c in range(chunks):
        keep_copy(c).wait()
        final_copy(c).wait()

        @pl.when(line < last)
        def _():
            right_copy(c).wait_send()

        @pl.when(line > 0)
        def _():
            left_copy(c).wait_send()

    for copy in second_state:
        copy.wait()


def exchange(owner_id, state_src, prefix, states):
    n = states.shape[0]
    any_spec = pl.BlockSpec(memory_space=pl.ANY)
    smem = pl.BlockSpec(memory_space=pltpu.SMEM)
    piece = pltpu.VMEM(prefix.shape[1:], prefix.dtype)
    chunks = prefix.shape[1]
    return pl.pallas_call(
        lambda *refs: exchange_kernel(n, *refs),
        in_specs=[smem, smem, any_spec, any_spec],
        out_specs=[any_spec] * 2,
        out_shape=[
            jax.ShapeDtypeStruct(prefix.shape, prefix.dtype),
            jax.ShapeDtypeStruct(states.shape, states.dtype),
        ],
        scratch_shapes=[
            pltpu.VMEM(states.shape, states.dtype),
            pltpu.VMEM(states.shape, states.dtype),
        ]
        + [piece] * 7
        + [
            pltpu.SemaphoreType.DMA((3, n)),
            pltpu.SemaphoreType.DMA((3, n)),
            pltpu.SemaphoreType.DMA((4, chunks)),
            pltpu.SemaphoreType.DMA((4, chunks)),
            pltpu.SemaphoreType.DMA((4 + chunks,)),
        ],
        compiler_params=pltpu.CompilerParams(collective_id=0, has_side_effects=True),
        cost_estimate=pl.CostEstimate(flops=40_000_000_000, bytes_accessed=100_000_000, transcendentals=0),
        name="exchange",
    )(owner_id, state_src, prefix, states)


def pack_states(ssm, conv, unit, width):
    rows = ssm.shape[0] + conv.shape[0]
    joined = jnp.pad(jnp.concatenate([ssm, conv], axis=0), ((0, -rows % unit), (0, 0)))
    return jnp.swapaxes(joined.reshape(joined.shape[0], -1, width), 0, 1)


def local(
    queries,
    new_kv,
    cached_lookup_pairs,
    prefix_ssm,
    prefix_conv,
    pool_kv,
    pool_ssm,
    pool_conv,
    owner_id,
    readers,
    restore_src,
    restore_blk,
    state_src,
    ctx_blocks,
    mamba_x,
    mamba_z,
    mamba_dt,
    dt_bias,
    a_log,
    bypass_gain,
    conv_w,
    conv_b,
    w_bc,
):
    block_len = pool_kv.shape[2]
    own_index = lax.axis_index("replica")
    my_sources = lax.dynamic_index_in_dim(restore_src, own_index, 0, keepdims=False)
    picked = jnp.sum(jnp.where(restore_src == own_index, restore_blk, 0), axis=1)
    send_kv = jnp.take(pool_kv[0], picked, axis=0, mode="clip")
    n, width, channels = restore_src.shape[0], cached_lookup_pairs.shape[2], pool_ssm.shape[2]
    length = cached_lookup_pairs.shape[1]
    pool_states = pack_states(pool_ssm[0], pool_conv[0], 8, channels // n)
    prefix_states = pack_states(prefix_ssm[0], prefix_conv[0], 16, width)
    groups, height = prefix_states.shape[:2]
    packed = jnp.concatenate([cached_lookup_pairs[0], prefix_states.reshape(-1, width)], axis=0)
    got_kv = lax.all_to_all(
        send_kv[:, None], "replica", split_axis=0, concat_axis=1, tiled=True
    )[0]
    shared, pool_states = exchange(
        owner_id, state_src, packed.reshape(2, CHUNKS, -1, width), pool_states
    )
    shared = shared.reshape(packed.shape)
    if groups == n:
        offset = length // height
        prefix_states = shared.reshape(-1, height, width)
    else:
        offset = 0
        prefix_states = shared[length:].reshape(groups, height, width)
        prefix_states = jnp.swapaxes(prefix_states, 0, 1).reshape(height, n, channels // n)
        prefix_states = jnp.swapaxes(prefix_states, 0, 1)
    reading = (readers > 0).astype(jnp.int32)
    signal, partial_bc = signal_call(
        reading, mamba_x, prefix_states, offset, pool_states, conv_w, conv_b[None], w_bc
    )
    state_bc = lax.psum(partial_bc, "channel")
    mamba_out = scan_call(
        reading, state_bc, signal, mamba_dt, mamba_z, dt_bias[None], a_log, bypass_gain[None],
        prefix_states, offset, pool_states
    )
    parts = length // block_len
    fresh_out = attend(
        0, queries, shared, block_len, lax.iota(jnp.int32, parts), reading * length, new_kv
    )
    got_kv, mamba_out, fresh_out = lax.optimization_barrier((got_kv, mamba_out, fresh_out))
    resumed_out = attend(
        1, queries, got_kv.reshape(-1, width), block_len, my_sources, ctx_blocks * block_len, new_kv
    )
    return (jnp.stack([fresh_out, resumed_out])[None], mamba_out)


def placed_specs():
    return (
        P(("groups", "replica"), None, None, "channel"),
        P(("groups", "replica"), None, None, "channel"),
        P(("groups", "replica"), None, "channel"),
        P(("groups", "replica"), None, "channel"),
        P(("groups", "replica"), None, "channel"),
        P(("groups", "replica"), None, None, "channel"),
        P(("groups", "replica"), None, "channel"),
        P(("groups", "replica"), None, "channel"),
        P("groups"),
        P(("groups", "replica")),
        P("groups", None),
        P("groups", None),
        P("groups"),
        P(("groups", "replica")),
        P(("groups", "replica"), None, None, "channel"),
        P(("groups", "replica"), None, None, "channel"),
        P(("groups", "replica"), None, None, "channel"),
        P("channel"),
        P(None, "channel"),
        P("channel"),
        P(None, "channel"),
        P("channel"),
        P("channel", None),
    )


def solution(mesh):
    return jax.shard_map(
        local,
        mesh=mesh,
        in_specs=placed_specs(),
        out_specs=(
            P(("groups", "replica"), None, None, "channel"),
            P(("groups", "replica"), None, None, "channel"),
        ),
        check_vma=False,
    )
```

```python
import jax
import jax.numpy as jnp
from jax import lax
from jax.experimental import pallas as pl
from jax.experimental.pallas import tpu as pltpu
from jax.sharding import PartitionSpec as P

HD = 128
Q_PER_KV = 8
CHUNKS = 4


def attend_kernel(parts, src_ref, live_ref, q_ref, *refs):
    ctx_refs, new_ref, out_ref = refs[:parts], refs[parts], refs[parts + 1]
    new_len = q_ref.shape[0]
    heads = new_ref.shape[1] // (2 * HD)
    factor = HD ** (-0.5)
    rows = Q_PER_KV * new_len
    live = live_ref[0]
    for head in range(heads):
        query = jnp.concatenate(
            [
                q_ref[:, (head * Q_PER_KV + g) * HD : (head * Q_PER_KV + g + 1) * HD]
                for g in range(Q_PER_KV)
            ],
            axis=0,
        )
        key_cols = slice(2 * head * HD, (2 * head + 1) * HD)
        value_cols = slice((2 * head + 1) * HD, (2 * head + 2) * HD)
        contract = (((1,), (1,)), ((), ()))
        scores = []
        start = 0
        for ref in ctx_refs:
            piece = (
                lax.dot_general(
                    query, ref[:, key_cols], contract, preferred_element_type=jnp.float32
                )
                * factor
            )
            position = start + lax.broadcasted_iota(jnp.int32, piece.shape, 1)
            scores.append(jnp.where(position < live, piece, -jnp.inf))
            start += ref.shape[0]
        fresh = (
            lax.dot_general(
                query, new_ref[:, key_cols], contract, preferred_element_type=jnp.float32
            )
            * factor
        )
        time = lax.rem(lax.broadcasted_iota(jnp.int32, fresh.shape, 0), new_len)
        fresh = jnp.where(
            time >= lax.broadcasted_iota(jnp.int32, fresh.shape, 1), fresh, -jnp.inf
        )
        highest = jnp.max(fresh, axis=1, keepdims=True)
        for piece in scores:
            highest = jnp.maximum(highest, jnp.max(piece, axis=1, keepdims=True))
        weight = jnp.exp(fresh - highest)
        total = jnp.sum(weight, axis=1, keepdims=True)
        mixed = jnp.dot(
            weight.astype(jnp.bfloat16),
            new_ref[:, value_cols],
            preferred_element_type=jnp.float32,
        )
        for piece, ref in zip(scores, ctx_refs):
            weight = jnp.exp(piece - highest)
            total = total + jnp.sum(weight, axis=1, keepdims=True)
            mixed = mixed + jnp.dot(
                weight.astype(jnp.bfloat16),
                ref[:, value_cols],
                preferred_element_type=jnp.float32,
            )
        result = (mixed / total).astype(out_ref.dtype)
        for g in range(Q_PER_KV):
            at = (head * Q_PER_KV + g) * HD
            out_ref[:, at : at + HD] = result[g * new_len : (g + 1) * new_len]


def attend(request, queries, blocks, block_len, source, live, new_kv):
    parts = source.shape[0]
    width = blocks.shape[1]
    _, _, new_len, q_width = queries.shape

    def pick(j):
        return pl.BlockSpec((block_len, width), lambda i, s, l: (s[j], 0))

    return pl.pallas_call(
        lambda *refs: attend_kernel(parts, *refs),
        grid_spec=pltpu.PrefetchScalarGridSpec(
            num_scalar_prefetch=2,
            grid=(1,),
            in_specs=[
                pl.BlockSpec((None, None, new_len, q_width), lambda i, s, l: (0, request, 0, 0))
            ]
            + [pick(j) for j in range(parts)]
            + [pl.BlockSpec((None, None, new_len, width), lambda i, s, l: (0, request, 0, 0))],
            out_specs=pl.BlockSpec((new_len, q_width), lambda i, s, l: (0, 0)),
        ),
        out_shape=jax.ShapeDtypeStruct((new_len, q_width), jnp.bfloat16),
        name="attend",
    )(source, live, queries, *([blocks] * parts), new_kv)


def signal_kernel(read_ref, x_ref, shared_ref, pool_ref, w_ref, b_ref, wbc_ref, sig_ref, bc_ref, pad):
    taps = w_ref.shape[0]
    new_len = x_ref.shape[1]
    reading = read_ref[0] > 0
    base = 8 - (taps - 1)
    start = wbc_ref.shape[1] // 2
    shared = shared_ref[...].astype(jnp.float32)[start : start + taps - 1]
    pad[0, base:8] = jnp.where(reading, shared, 0.0)
    pad[1, base:8] = pool_ref[...].astype(jnp.float32)[start : start + taps - 1]

    @pl.when(pl.program_id(0) == 0)
    def _():
        bc_ref[...] = jnp.zeros_like(bc_ref)

    for r in range(2):
        pad[r, 8 : 8 + new_len] = x_ref[r].astype(jnp.float32)
        total = b_ref[...] + w_ref[0:1] * pad[r, base : base + new_len]
        for k in range(1, taps):
            total = total + w_ref[k : k + 1] * pad[r, base + k : base + k + new_len]
        signal = total * jax.nn.sigmoid(total)
        sig_ref[r] = signal
        bc_ref[r] += jnp.dot(
            signal.astype(jnp.bfloat16), wbc_ref[...], preferred_element_type=jnp.float32
        )


def signal_call(reading, x, shared, offset, pool, w, b, wbc):
    _, _, new_len, channels = x.shape
    taps, cols = w.shape[0], wbc.shape[1]
    chunk = pool.shape[2]
    return pl.pallas_call(
        signal_kernel,
        grid_spec=pltpu.PrefetchScalarGridSpec(
            num_scalar_prefetch=1,
            grid=(channels // chunk,),
            in_specs=[
                pl.BlockSpec((None, 2, new_len, chunk), lambda i, s: (0, 0, 0, i)),
                pl.BlockSpec((None, shared.shape[1], chunk), lambda i, s: (offset + i, 0, 0)),
                pl.BlockSpec((None, pool.shape[1], chunk), lambda i, s: (i, 0, 0)),
                pl.BlockSpec((taps, chunk), lambda i, s: (0, i)),
                pl.BlockSpec((1, chunk), lambda i, s: (0, i)),
                pl.BlockSpec((chunk, cols), lambda i, s: (i, 0)),
            ],
            out_specs=[
                pl.BlockSpec((2, new_len, chunk), lambda i, s: (0, 0, i)),
                pl.BlockSpec((2, new_len, cols), lambda i, s: (0, 0, 0)),
            ],
            scratch_shapes=[pltpu.VMEM((2, 8 + new_len, chunk), jnp.float32)],
        ),
        out_shape=[
            jax.ShapeDtypeStruct((2, new_len, channels), jnp.float32),
            jax.ShapeDtypeStruct((2, new_len, cols), jnp.float32),
        ],
        cost_estimate=pl.CostEstimate(flops=6_000_000_000, bytes_accessed=20_000_000, transcendentals=0),
        name="signal",
    )(reading, x, shared, pool, w, b, wbc)


def scan_kernel(
    read_ref, bc_ref, sig_ref, dt_ref, z_ref, bias_ref, alog_ref, gain_ref, shared_ref, pool_ref,
    out_ref, spread, step_buf, push_buf, scan_buf
):
    states, chunk = alog_ref.shape
    new_len = sig_ref.shape[1]

    @pl.when(pl.program_id(0) == 0)
    def _():
        for r in range(2):
            columns = bc_ref[r].T
            for t in range(new_len):
                spread[r, t] = jnp.broadcast_to(columns[:, t : t + 1], spread.shape[2:])

    decay = -jnp.exp(alog_ref[...])
    hidden = []
    for r in range(2):
        x = dt_ref[r].astype(jnp.float32) + bias_ref[...]
        step = jnp.maximum(x, 0.0) + jnp.log1p(jnp.exp(-jnp.abs(x)))
        step_buf[r] = step
        push_buf[r] = step * sig_ref[r]
    hidden = (
        jnp.where(read_ref[0] > 0, shared_ref[...].astype(jnp.float32)[:states], 0.0),
        pool_ref[...].astype(jnp.float32)[:states],
    )
    tiles = chunk // HD
    for t in range(new_len):
        state = []
        for r in range(2):
            now = jnp.broadcast_to(step_buf[r, t : t + 1], (states, chunk))
            push = jnp.broadcast_to(push_buf[r, t : t + 1], (states, chunk))
            both = spread[r, t]
            gain = jnp.concatenate([both[:states]] * tiles, axis=1)
            read = jnp.concatenate([both[states:]] * tiles, axis=1)
            new = jnp.exp(now * decay) * hidden[r] + gain * push
            scan_buf[r, t : t + 1] = jnp.sum(read * new, axis=0, keepdims=True)
            state.append(new)
        hidden = tuple(state)
    for r in range(2):
        z = z_ref[r].astype(jnp.float32)
        full = scan_buf[r] + gain_ref[...] * sig_ref[r]
        out_ref[r] = (full * (z * jax.nn.sigmoid(z))).astype(out_ref.dtype)


def scan_call(reading, bc, signal, dt, z, bias, alog, gain, shared, offset, pool):
    _, new_len, channels = signal.shape
    states, cols = alog.shape[0], bc.shape[2]
    chunk = pool.shape[2]
    row = pl.BlockSpec((1, chunk), lambda i, s: (0, i))
    state = pl.BlockSpec((states, chunk), lambda i, s: (0, i))
    seq = pl.BlockSpec((None, 2, new_len, chunk), lambda i, s: (0, 0, 0, i))
    return pl.pallas_call(
        scan_kernel,
        grid_spec=pltpu.PrefetchScalarGridSpec(
            num_scalar_prefetch=1,
            grid=(channels // chunk,),
            in_specs=[
                pl.BlockSpec((2, new_len, cols), lambda i, s: (0, 0, 0)),
                pl.BlockSpec((2, new_len, chunk), lambda i, s: (0, 0, i)),
                seq,
                seq,
                row,
                state,
                row,
                pl.BlockSpec((None, shared.shape[1], chunk), lambda i, s: (offset + i, 0, 0)),
                pl.BlockSpec((None, pool.shape[1], chunk), lambda i, s: (i, 0, 0)),
            ],
            out_specs=pl.BlockSpec((None, 2, new_len, chunk), lambda i, s: (0, 0, 0, i)),
            scratch_shapes=[
                pltpu.VMEM((2, new_len, cols, HD), jnp.float32),
                pltpu.VMEM((2, new_len, chunk), jnp.float32),
                pltpu.VMEM((2, new_len, chunk), jnp.float32),
                pltpu.VMEM((2, new_len, chunk), jnp.float32),
            ],
        ),
        out_shape=jax.ShapeDtypeStruct((1, 2, new_len, channels), jnp.bfloat16),
        cost_estimate=pl.CostEstimate(flops=10_000_000_000, bytes_accessed=30_000_000, transcendentals=0),
        name="scan",
    )(reading, bc, signal, dt, z, bias, alog, gain, shared, pool)


def exchange_kernel(
    n, owner_ref, holder_ref, prefix_ref, state_ref, shared_ref, states_ref,
    state_cand, state_send, own, side, rightward, leftward, to_right, to_left, final,
    sends, recvs, chain_sends, chain_recvs, local_sems
):
    me = lax.axis_index("replica")
    chunks = prefix_ref.shape[1]
    line, half = me // 2, lax.rem(me, 2)
    length = n // 2
    last = length - 1
    partner = line * 2 + 1 - half
    owner = owner_ref[0]
    owner_line = owner // 2
    barrier = pltpu.get_barrier_semaphore()
    for s in range(1, n):
        pl.semaphore_signal(
            barrier, inc=1, device_id={"replica": lax.rem(me + s, n)}, device_id_type=pl.DeviceIdType.MESH
        )

    def remote(source, target, send_sem, recv_sem, peer):
        return pltpu.make_async_remote_copy(
            src_ref=source,
            dst_ref=target,
            send_sem=send_sem,
            recv_sem=recv_sem,
            device_id={"replica": peer},
            device_id_type=pl.DeviceIdType.MESH,
        )

    def spread(kind, s, source, target):
        return remote(
            source, target, sends.at[kind, s], recvs.at[kind, s], lax.rem(me + s, n)
        )

    def chain(kind, c, source, target, peer):
        return remote(source, target, chain_sends.at[kind, c], chain_recvs.at[kind, c], peer)

    own_prefix = pltpu.make_async_copy(prefix_ref.at[half], own, local_sems.at[0])
    own_state = pltpu.make_async_copy(state_ref.at[me], state_cand.at[me], local_sems.at[1])
    own_prefix.start()
    own_state.start()
    pl.semaphore_wait(barrier, n - 1)

    first_state, second_state, sideways = [], [], []
    for s in range(1, n):
        copy = spread(0, s, state_ref.at[lax.rem(me + s, n)], state_cand.at[me])
        copy.start()
        first_state.append(copy)
    for c in range(chunks):
        copy = chain(0, c, prefix_ref.at[1 - half, c], side.at[c], partner)
        copy.start()
        sideways.append(copy)

    own_state.wait()
    for copy in first_state:
        copy.wait()
    for d in range(n):
        state_send[d] = state_cand[holder_ref[d]]
    for s in range(1, n):
        copy = spread(2, s, state_send.at[lax.rem(me + s, n)], states_ref.at[me])
        copy.start()
        second_state.append(copy)
    mine_state = pltpu.make_async_copy(state_send.at[me], states_ref.at[me], local_sems.at[3])
    mine_state.start()
    own_prefix.wait()

    def right_copy(c):
        return chain(1, c, to_right.at[c], rightward.at[c], lax.rem(me + 2, n))

    def left_copy(c):
        return chain(2, c, to_left.at[c], leftward.at[c], lax.rem(me + n - 2, n))

    def final_copy(c):
        return chain(3, c, final.at[c], shared_ref.at[half, c], partner)

    def keep_copy(c):
        return pltpu.make_async_copy(final.at[c], shared_ref.at[half, c], local_sems.at[4 + c])

    def here(c):
        return jnp.where(owner == me, own[c], side[c])

    near, far = jnp.minimum(line, last - line), jnp.maximum(line, last - line)
    steps = chunks + length - 1
    for t in range(steps):
        c_near, c_right, c_left, c_far = t - near, t - line, t - (last - line), t - far

        @pl.when((c_near >= 0) & (c_near < chunks))
        def _():
            chain(0, c_near, side.at[c_near], side.at[c_near], partner).wait_recv()

        @pl.when((c_right >= 0) & (c_right < chunks))
        def _():
            @pl.when(line > 0)
            def _():
                right_copy(c_right).wait_recv()

            @pl.when(line < last)
            def _():
                to_right[c_right] = jnp.where(
                    owner_line == line, here(c_right), rightward[c_right]
                )
                right_copy(c_right).start()

        @pl.when((c_left >= 0) & (c_left < chunks))
        def _():
            @pl.when(line < last)
            def _():
                left_copy(c_left).wait_recv()

            @pl.when(line > 0)
            def _():
                to_left[c_left] = jnp.where(owner_line == line, here(c_left), leftward[c_left])
                left_copy(c_left).start()

        @pl.when((c_far >= 0) & (c_far < chunks))
        def _():
            final[c_far] = jnp.where(
                owner_line == line,
                here(c_far),
                jnp.where(owner_line < line, rightward[c_far], leftward[c_far]),
            )
            final_copy(c_far).start()
            keep_copy(c_far).start()

    mine_state.wait()
    for copy in sideways:
        copy.wait_send()
    for c in range(chunks):
        keep_copy(c).wait()
        final_copy(c).wait()

        @pl.when(line < last)
        def _():
            right_copy(c).wait_send()

        @pl.when(line > 0)
        def _():
            left_copy(c).wait_send()

    for copy in second_state:
        copy.wait()


def exchange(owner_id, state_src, prefix, states):
    n = states.shape[0]
    any_spec = pl.BlockSpec(memory_space=pl.ANY)
    smem = pl.BlockSpec(memory_space=pltpu.SMEM)
    piece = pltpu.VMEM(prefix.shape[1:], prefix.dtype)
    chunks = prefix.shape[1]
    return pl.pallas_call(
        lambda *refs: exchange_kernel(n, *refs),
        in_specs=[smem, smem, any_spec, any_spec],
        out_specs=[any_spec] * 2,
        out_shape=[
            jax.ShapeDtypeStruct(prefix.shape, prefix.dtype),
            jax.ShapeDtypeStruct(states.shape, states.dtype),
        ],
        scratch_shapes=[
            pltpu.VMEM(states.shape, states.dtype),
            pltpu.VMEM(states.shape, states.dtype),
        ]
        + [piece] * 7
        + [
            pltpu.SemaphoreType.DMA((3, n)),
            pltpu.SemaphoreType.DMA((3, n)),
            pltpu.SemaphoreType.DMA((4, chunks)),
            pltpu.SemaphoreType.DMA((4, chunks)),
            pltpu.SemaphoreType.DMA((4 + chunks,)),
        ],
        compiler_params=pltpu.CompilerParams(collective_id=0, has_side_effects=True),
        cost_estimate=pl.CostEstimate(flops=40_000_000_000, bytes_accessed=100_000_000, transcendentals=0),
        name="exchange",
    )(owner_id, state_src, prefix, states)


def pack_states(ssm, conv, unit, width):
    rows = ssm.shape[0] + conv.shape[0]
    joined = jnp.pad(jnp.concatenate([ssm, conv], axis=0), ((0, -rows % unit), (0, 0)))
    return jnp.swapaxes(joined.reshape(joined.shape[0], -1, width), 0, 1)


def local(
    queries,
    new_kv,
    cached_lookup_pairs,
    prefix_ssm,
    prefix_conv,
    pool_kv,
    pool_ssm,
    pool_conv,
    owner_id,
    readers,
    restore_src,
    restore_blk,
    state_src,
    ctx_blocks,
    mamba_x,
    mamba_z,
    mamba_dt,
    dt_bias,
    a_log,
    bypass_gain,
    conv_w,
    conv_b,
    w_bc,
):
    block_len = pool_kv.shape[2]
    own_index = lax.axis_index("replica")
    my_sources = lax.dynamic_index_in_dim(restore_src, own_index, 0, keepdims=False)
    picked = jnp.sum(jnp.where(restore_src == own_index, restore_blk, 0), axis=1)
    send_kv = jnp.take(pool_kv[0], picked, axis=0, mode="clip")
    n, width, channels = restore_src.shape[0], cached_lookup_pairs.shape[2], pool_ssm.shape[2]
    length = cached_lookup_pairs.shape[1]
    pool_states = pack_states(pool_ssm[0], pool_conv[0], 8, channels // n)
    prefix_states = pack_states(prefix_ssm[0], prefix_conv[0], 16, width)
    groups, height = prefix_states.shape[:2]
    packed = jnp.concatenate([cached_lookup_pairs[0], prefix_states.reshape(-1, width)], axis=0)
    shared, pool_states = exchange(
        owner_id, state_src, packed.reshape(2, CHUNKS, -1, width), pool_states
    )
    send_kv, shared, pool_states = lax.optimization_barrier((send_kv, shared, pool_states))
    got_kv = lax.all_to_all(
        send_kv[:, None], "replica", split_axis=0, concat_axis=1, tiled=True
    )[0]
    shared = shared.reshape(packed.shape)
    if groups == n:
        offset = length // height
        prefix_states = shared.reshape(-1, height, width)
    else:
        offset = 0
        prefix_states = shared[length:].reshape(groups, height, width)
        prefix_states = jnp.swapaxes(prefix_states, 0, 1).reshape(height, n, channels // n)
        prefix_states = jnp.swapaxes(prefix_states, 0, 1)
    reading = (readers > 0).astype(jnp.int32)
    signal, partial_bc = signal_call(
        reading, mamba_x, prefix_states, offset, pool_states, conv_w, conv_b[None], w_bc
    )
    state_bc = lax.psum(partial_bc, "channel")
    mamba_out = scan_call(
        reading, state_bc, signal, mamba_dt, mamba_z, dt_bias[None], a_log, bypass_gain[None],
        prefix_states, offset, pool_states
    )
    parts = length // block_len
    fresh_out = attend(
        0, queries, shared, block_len, lax.iota(jnp.int32, parts), reading * length, new_kv
    )
    got_kv, mamba_out, fresh_out = lax.optimization_barrier((got_kv, mamba_out, fresh_out))
    resumed_out = attend(
        1, queries, got_kv.reshape(-1, width), block_len, my_sources, ctx_blocks * block_len, new_kv
    )
    return (jnp.stack([fresh_out, resumed_out])[None], mamba_out)


def placed_specs():
    return (
        P(("groups", "replica"), None, None, "channel"),
        P(("groups", "replica"), None, None, "channel"),
        P(("groups", "replica"), None, "channel"),
        P(("groups", "replica"), None, "channel"),
        P(("groups", "replica"), None, "channel"),
        P(("groups", "replica"), None, None, "channel"),
        P(("groups", "replica"), None, "channel"),
        P(("groups", "replica"), None, "channel"),
        P("groups"),
        P(("groups", "replica")),
        P("groups", None),
        P("groups", None),
        P("groups"),
        P(("groups", "replica")),
        P(("groups", "replica"), None, None, "channel"),
        P(("groups", "replica"), None, None, "channel"),
        P(("groups", "replica"), None, None, "channel"),
        P("channel"),
        P(None, "channel"),
        P("channel"),
        P(None, "channel"),
        P("channel"),
        P("channel", None),
    )


def solution(mesh):
    return jax.shard_map(
        local,
        mesh=mesh,
        in_specs=placed_specs(),
        out_specs=(
            P(("groups", "replica"), None, None, "channel"),
            P(("groups", "replica"), None, None, "channel"),
        ),
        check_vma=False,
    )
```
